32 devices in a mesh: grp: 2 (over y), ep: 8 (over z, x), seq: 1, rep: 2 (over core).
Axes of the slice: x: 2, y: 2, z: 4, core: 2. Of those that a mesh axis runs over, the one named last changes fastest.
Arguments:
- hidden_in: bfloat16 [1024, 2048], P(('grp', 'ep', 'rep'), 'seq'), parts along dimension 0, may hold values from -64 to 64
- row_counts: int32 [32], P(('grp', 'ep', 'rep')), parts along dimension 0, may hold values from 24 to 32, as said below
- qkv_new: bfloat16 [1024, 3, 2048], P(('grp', 'ep', 'rep')), parts along dimension 0, may hold values from -6 to 6
- cache_len: int32 [16, 64], P('grp', ('rep', 'seq')), parts along dimension 0, may hold values from 1 to 128, as said below
- kv_cache: bfloat16 [2, 16, 64, 128, 2048], P(None, 'grp', ('rep', 'seq'), None, 'ep'), parts along dimension 1, may hold values from -128 to 128
- w_out: bfloat16 [2048, 2048], P('ep', 'seq'), may hold values from -0.125 to 0.125
- moe_gain: float32 [2048], replicated, may hold values from 0.1 to 1.9
- w_in: bfloat16 [16, 2048, 2, 1408], P(('ep', 'rep'), None, None, 'seq'), may hold values from -0.125 to 0.125
- w_down: bfloat16 [16, 1408, 2048], P(('ep', 'rep'), 'seq'), may hold values from -0.15625 to 0.15625
- route_ids: int32 [1024, 6], P(('grp', 'ep', 'rep')), parts along dimension 0, may hold values from 0 to 15, all different within a row; in each aligned block of 32 rows (0 to 31, 32 to 63, ...) at most 24 rows name the same one
- route_weight: bfloat16 [1024, 6], P(('grp', 'ep', 'rep')), parts along dimension 0, may hold values from 0.049804688 to 0.44921875
Outputs:
- mixed: bfloat16 [1024, 2048], P(('grp', 'ep', 'rep'), 'seq'), parts along dimension 0
The draws below stay inside these ranges and needn't reach their ends.
There are 2 independent parts, one for each index of `grp`. The reference program is written for one: setup_inputs(seed, part) draws one part's arguments, and reference() takes and returns one part's arrays. A program takes and returns all parts, laid end to end along the dimension named above; an argument that names none is the same for every part. Nothing has to cross between parts.
Inputs may be any that keep to these rules, and one draw needn't show every extreme that they name: The first row_counts[b] slots of block b are live; some block is full. `cache_len`: some row has 128 cached positions. `route_ids`: a row's 6 experts differ; among the 32 rows of one block no expert is named by more than 24 rows, and in some block one is named by exactly 24.
All inputs are finite; a program needn't handle non-finite values.
Results may differ from the reference program's by a relative error of at most 0.0053.
Values may be sent and summed in bfloat16 or wider, within the bound.
A program may use at most 192 MiB of HBM per device.

```python
import math
import jax
import jax.numpy as jnp
import numpy as np
from jax import lax

D = 2048
FF = 1408
HEADS = 16
HEAD_DIM = 128
TOPK = 6
RB = 32
L = 128
ROWS = 512
EXPERTS = 16
CAP = 24
N_EP = 8
N_REP = 2


def make_lengths(key):
    part_keys = jax.random.split(jax.random.fold_in(key, 5), 2)
    lengths = jax.random.randint(part_keys[0], (ROWS,), 1, L + 1)
    longest_row = jax.random.randint(part_keys[1], (), 0, ROWS)
    return jnp.where(jnp.arange(ROWS) == longest_row, L, lengths).astype(jnp.int32)


def make_fresh(key):
    fresh_key = jax.random.fold_in(key, 7)
    drawn = jax.random.truncated_normal(fresh_key, -6.0, 6.0, (ROWS, 3, HEADS * HEAD_DIM), jnp.float32)
    return drawn


def draw_hidden_in(key, part):
    part_keys = jax.random.split(jax.random.fold_in(key, 11), 2)
    base_draw = jax.random.truncated_normal(part_keys[0], -6.0, 6.0, (ROWS, D), jnp.float32)
    column_scale = jnp.exp(jax.random.uniform(part_keys[1], (D,), jnp.float32, 0.0, math.log(10.0))) / 4.0
    column_ramp = 1.0 + 2.0 * jnp.arange(D, dtype=jnp.float32) / D
    drawn = base_draw * column_scale * jnp.sqrt(column_ramp)
    return jnp.clip(drawn, -60.0, 60.0).astype(jnp.bfloat16)


def draw_row_counts(key, part):
    part_keys = jax.random.split(jax.random.fold_in(key, 3), 2)
    blocks = N_EP * N_REP
    counts = jax.random.randint(part_keys[0], (blocks,), RB - RB // 4, RB + 1)
    full_block = jax.random.randint(part_keys[1], (), 0, blocks)
    return jnp.where(jnp.arange(blocks) == full_block, RB, counts).astype(jnp.int32)


def draw_qkv_new(key, part):
    return make_fresh(key).astype(jnp.bfloat16)


def draw_cache_len(key, part):
    return make_lengths(key).reshape(N_EP, N_REP * RB)


def draw_kv_cache(key, part):
    head_width = HEADS * HEAD_DIM
    part_keys = jax.random.split(jax.random.fold_in(key, 9), 2)
    cache_keys = jax.random.truncated_normal(part_keys[0], -6.0, 6.0, (ROWS, L, head_width), jnp.float32)
    cache_values = 2.0 * jax.random.truncated_normal(part_keys[1], -6.0, 6.0, (ROWS, L, head_width), jnp.float32)
    stacked = jnp.stack([cache_keys, cache_values]).reshape(2, N_EP, N_REP * RB, L, head_width)
    return jnp.clip(stacked, -128.0, 128.0).astype(jnp.bfloat16)


def level_of(key, shape, shards, least, high):
    factor_of, own = 1.0, jax.random.fold_in(key, 6)
    for dim, blocks in shards:
        steps = jnp.exp(jax.random.uniform(jax.random.fold_in(own, dim), (blocks,), jnp.float32, least / len(shards), high / len(shards)))
        factor_of = factor_of * jnp.repeat(steps, shape[dim] // blocks).reshape([-1 if axis == dim else 1 for axis in range(len(shape))])
    return factor_of


def shared_out(key, own, number, rows, number_of, top, limit, slope):
    ranking = jax.random.permutation(key, number_of)
    packed, usual = portions_of(number_of, rows * top, limit, slope, True), portions_of(number_of, rows * top, limit, slope, False)
    places = jnp.arange(number_of)

    def named(tallies, turn):
        used = int((tallies > 0).sum())
        fixed = max(1, used // 4)
        moved = fixed + (places - fixed + turn * (used - fixed)) % max(1, number_of - fixed)
        return jnp.zeros((number_of,), jnp.int32).at[ranking[jnp.where(places < fixed, places, moved)]].set(jnp.asarray(tallies, jnp.int32))

    tallies = jnp.where(number % 4 == 0, named(packed, number // 4), named(usual, number - number // 4 - 1))
    mixed = jax.random.permutation(jax.random.fold_in(own, 3), number_of)
    source_of, taker = mixed[0:number_of // 2 * 2:2], mixed[1:number_of // 2 * 2:2]
    margin = jnp.minimum(tallies[source_of] - 1, limit - tallies[taker]) // 2
    margin = jnp.where((source_of == ranking[0]) | (taker == ranking[0]) | (tallies[taker] == 0), 0, jnp.maximum(margin, 0))
    moved = jax.random.randint(jax.random.fold_in(own, 4), (number_of // 2,), 0, 1 << 20) % (margin + 1)
    tallies = tallies.at[source_of].add(-moved).at[taker].add(moved)
    items = jnp.searchsorted(jnp.cumsum(tallies), jnp.arange(rows * top), side="right").astype(jnp.int32)
    listing = items.reshape(top, rows).T
    listing = listing[jax.random.permutation(jax.random.fold_in(own, 1), rows)]
    turn = jax.random.randint(jax.random.fold_in(own, 2), (rows, 1), 0, top)
    return jnp.take_along_axis(listing, (jnp.arange(top)[None, :] + turn) % top, axis=1)


def portions_of(count, total, limit, slope, full):
    weights = [(1 << 20) // math.isqrt(rank ** slope) + 1 for rank in range(1, count + 1)]
    largest = limit if full else min(limit, max(-(-total // count), total * weights[0] // sum(weights)))
    least = 1 if total - largest >= count - 1 else 0
    given, rest = [largest] + [least] * (count - 1), total - largest - least * (count - 1)
    while rest > 0:
        free = [i for i in range(1, count) if given[i] < largest] or [i for i in range(1, count) if given[i] < limit]
        mass, remaining = sum([weights[i] for i in free]), rest
        for i in free:
            more = min(limit - given[i], max(1, remaining * weights[i] // mass), rest)
            given[i] = given[i] + more
            rest = rest - more
    return np.array(given)


def scatter_about(rng, dims, deviation, limit, cuts=(), kind=jnp.bfloat16):
    values = deviation * jax.random.normal(rng, dims, jnp.float32)
    if cuts:
        values = values * level_of(rng, dims, cuts, -0.22, 0.18)
    return jnp.clip(values, -limit, limit).astype(kind)


def setup_inputs(seed: int = 0, part: int = 0) -> dict:
    seeds = jax.random.split(jax.random.key(seed), 12)
    own_keys = jax.random.split(jax.random.fold_in(seeds[11], part), 12)
    hidden_in = draw_hidden_in(jax.random.fold_in(jax.random.fold_in(seeds[11], part), 71), part)
    row_counts = draw_row_counts(jax.random.fold_in(jax.random.fold_in(seeds[11], part), 71), part)
    qkv_new = draw_qkv_new(jax.random.fold_in(jax.random.fold_in(seeds[11], part), 71), part)
    cache_len = draw_cache_len(jax.random.fold_in(jax.random.fold_in(seeds[11], part), 71), part)
    kv_cache = draw_kv_cache(jax.random.fold_in(jax.random.fold_in(seeds[11], part), 71), part)
    w_out = scatter_about(seeds[5], (HEADS * HEAD_DIM, D), (HEADS * HEAD_DIM) ** -0.5, 0.125, ((0, 8),))
    moe_gain = jnp.clip(1.0 + 0.18 * jax.random.normal(seeds[6], (D,), jnp.float32), 0.1, 1.9)
    w_in = scatter_about(seeds[7], (EXPERTS, D, 2, FF), D ** -0.5, 0.125, ((0, 16),))
    w_down = scatter_about(seeds[8], (EXPERTS, FF, D), FF ** -0.5, 0.15625, ((0, 16),))
    route_ids_keys = jax.random.split(jax.random.fold_in(own_keys[9], 1), ROWS // RB)
    route_ids_turns = jax.random.permutation(jax.random.fold_in(own_keys[9], 3), ROWS // RB)
    route_ids = jax.vmap(lambda own, number: shared_out(jax.random.fold_in(own_keys[9], 2), own, number, RB, EXPERTS, TOPK, CAP, 2))(route_ids_keys, route_ids_turns).reshape((ROWS, TOPK))
    route_weight = jnp.clip(0.049804688 + 0.39941406 * jax.random.uniform(own_keys[10], (ROWS, TOPK), jnp.float32) ** level_of(own_keys[10], (ROWS, TOPK), ((0, 16),), -0.2, 0.2), 0.049804688, 0.44921875).astype(jnp.bfloat16)
    return {"hidden_in": hidden_in, "row_counts": row_counts, "qkv_new": qkv_new, "cache_len": cache_len, "kv_cache": kv_cache, "w_out": w_out, "moe_gain": moe_gain, "w_in": w_in, "w_down": w_down, "route_ids": route_ids, "route_weight": route_weight}


epsilon = 1e-06
masked_score = -1e+30

def reference(hidden_in, row_counts, qkv_new, cache_len, kv_cache, w_out, moe_gain, w_in, w_down, route_ids, route_weight):
    head_width = HEADS * HEAD_DIM
    blocks = N_EP * N_REP
    row_index = jnp.arange(ROWS, dtype=jnp.int32)
    block_of = row_index // RB
    counts_row = lax.optimization_barrier(jnp.sum(jnp.where(block_of[:, None] == jnp.arange(blocks, dtype=jnp.int32)[None, :], row_counts[None, :], 0), axis=1))
    is_live = row_index % RB < counts_row
    lengths = cache_len.reshape(ROWS)
    score_scale = 1.0 / math.sqrt(HEAD_DIM)
    fresh_rows = qkv_new.astype(jnp.float32).reshape(ROWS, 3, HEADS, HEAD_DIM)
    queries = fresh_rows[:, 0]
    own_score = lax.optimization_barrier(jnp.sum(queries * fresh_rows[:, 1], axis=2)) * score_scale
    cached = kv_cache.reshape(2, ROWS // RB, RB, L, HEADS, HEAD_DIM)
    group_count = ROWS // RB

    def attend_block(inputs):
        query_rows, key_rows, value_rows, length_rows, own_rows, value_fresh = inputs
        scores = jnp.einsum('bhd,blhd->bhl', query_rows, key_rows.astype(jnp.float32), precision=lax.Precision.HIGHEST) * score_scale
        position = jnp.arange(L, dtype=jnp.int32)
        in_cache = position[None, None, :] < length_rows[:, None, None]
        scores = jnp.where(in_cache, scores, masked_score)
        highest = jnp.maximum(lax.optimization_barrier(jnp.max(scores, axis=2)), own_rows)
        weights = jnp.where(in_cache, jnp.exp(scores - highest[..., None]), 0.0)
        rounded = lax.optimization_barrier(weights.astype(jnp.bfloat16)).astype(jnp.float32)
        own_weight = jnp.exp(own_rows - highest)
        denominator = lax.optimization_barrier(jnp.sum(weights, axis=2)) + own_weight
        summed = jnp.einsum('bhl,blhd->bhd', rounded, value_rows.astype(jnp.float32), precision=lax.Precision.HIGHEST) + own_weight[..., None] * value_fresh
        return summed / denominator[..., None]
    attended = lax.map(attend_block, (queries.reshape(group_count, RB, HEADS, HEAD_DIM), cached[0], cached[1], lengths.reshape(group_count, RB), own_score.reshape(group_count, RB, HEADS), fresh_rows[:, 2].reshape(group_count, RB, HEADS, HEAD_DIM)))
    attended = attended.reshape(ROWS, head_width).astype(jnp.bfloat16)
    attn_out = jnp.dot(attended, w_out, preferred_element_type=jnp.float32)
    residual = (hidden_in.astype(jnp.float32) + attn_out).astype(jnp.bfloat16)
    residual_wide = lax.optimization_barrier(residual).astype(jnp.float32)
    inverse_rms = lax.rsqrt(lax.optimization_barrier(jnp.mean(residual_wide * residual_wide, axis=1)) + epsilon)
    normed = (residual_wide * inverse_rms[:, None] * moe_gain).astype(jnp.bfloat16)
    expert_ids = jnp.arange(EXPERTS, dtype=jnp.int32)
    named_hits = (route_ids[:, :, None] == expert_ids[None, None, :]) & is_live[:, None, None]
    coeffs = lax.optimization_barrier(jnp.sum(jnp.where(named_hits, route_weight.astype(jnp.float32)[:, :, None], 0.0), axis=1))
    chosen = jnp.any(named_hits, axis=1)
    slot_limit = EXPERTS * CAP

    def one_expert(running, expert):
        order_key = jnp.where(chosen[:, expert], row_index, row_index + ROWS)
        picked = jnp.argsort(order_key)[:slot_limit].astype(jnp.int32)
        rows_in = normed[picked]
        weight_in = lax.dynamic_index_in_dim(w_in, expert, 0, keepdims=False).reshape(D, 2 * FF)
        gate_up = jnp.dot(rows_in, weight_in, preferred_element_type=jnp.float32).reshape(slot_limit, 2, FF)
        hidden_units = (jax.nn.silu(gate_up[:, 0]) * gate_up[:, 1]).astype(jnp.bfloat16)
        weight_down = lax.dynamic_index_in_dim(w_down, expert, 0, keepdims=False)
        produced = jnp.dot(hidden_units, weight_down, preferred_element_type=jnp.float32).astype(jnp.bfloat16)
        produced = lax.optimization_barrier(produced).astype(jnp.float32)
        factor = coeffs[picked, expert]
        return (running.at[picked].add(factor[:, None] * produced), None)
    moe_out, _ = lax.scan(one_expert, jnp.zeros((ROWS, D), jnp.float32), expert_ids)
    mixed = jnp.where(is_live[:, None], residual_wide + moe_out, 0.0).astype(jnp.bfloat16)
    return mixed
```

```python
import functools
import math

import jax
import jax.numpy as jnp
from jax import lax
from jax.experimental import pallas as pl
from jax.experimental.pallas import tpu as pltpu
from jax.sharding import PartitionSpec as P

D = 2048
HEAD_DIM = 128
TOPK = 6


epsilon = 1e-06
masked_score = -1e30


def local(
    hidden_in,
    row_counts,
    qkv_new,
    cache_len,
    kv_cache,
    w_out,
    moe_gain,
    w_in,
    w_down,
    route_ids,
    route_weight,
):
    tok_rows, feat_local = hidden_in.shape
    owners = lax.axis_size("ep")
    parts_seq = lax.axis_size("seq")
    width_local = kv_cache.shape[-1]
    heads_local = width_local // HEAD_DIM
    positions = kv_cache.shape[3]
    share_rows = tok_rows // parts_seq
    attend_rows = owners * share_rows
    moved_block = lax.all_to_all(qkv_new, "ep", split_axis=2, concat_axis=0, tiled=True)
    moved_block = moved_block.reshape(owners, tok_rows, 3, width_local)
    heads_block = lax.dynamic_slice_in_dim(
        moved_block, lax.axis_index("seq") * share_rows, share_rows, 1
    )
    heads_block = heads_block.reshape(attend_rows, 3, heads_local, HEAD_DIM)
    queries = heads_block[:, 0]
    key_new = heads_block[:, 1].astype(jnp.float32)
    value_new = heads_block[:, 2].astype(jnp.float32)
    lengths = cache_len.reshape(attend_rows)
    cache_keys = kv_cache[0].reshape(attend_rows, positions, heads_local, HEAD_DIM)
    cache_values = kv_cache[1].reshape(attend_rows, positions, heads_local, HEAD_DIM)
    score_scale = 1.0 / math.sqrt(HEAD_DIM)
    position = jnp.arange(positions, dtype=jnp.int32)
    in_cache = position[None, None, :] < lengths[:, None, None]
    scores = (
        jnp.einsum("nhd,nphd->nhp", queries, cache_keys, preferred_element_type=jnp.float32)
        * score_scale
    )
    scores = jnp.where(in_cache, scores, masked_score)
    own_score = jnp.sum(queries.astype(jnp.float32) * key_new, axis=2) * score_scale
    highest = jnp.maximum(jnp.max(scores, axis=2), own_score)
    weights = jnp.where(in_cache, jnp.exp(scores - highest[..., None]), 0.0)
    partial_sum = jnp.einsum(
        "nhp,nphd->nhd",
        weights.astype(jnp.bfloat16),
        cache_values,
        preferred_element_type=jnp.float32,
    )
    own_weight = jnp.exp(own_score - highest)
    attended = (partial_sum + own_weight[..., None] * value_new) / (
        jnp.sum(weights, axis=2) + own_weight
    )[..., None]
    attended = attended.astype(jnp.bfloat16).reshape(owners, share_rows, width_local)
    attended = lax.all_gather(attended, "seq", axis=1, tiled=True).reshape(
        owners * tok_rows, width_local
    )
    attn_out = lax.psum_scatter(
        jnp.dot(attended, w_out, preferred_element_type=jnp.float32),
        "ep",
        scatter_dimension=0,
        tiled=True,
    )
    residual = (hidden_in.astype(jnp.float32) + attn_out).astype(jnp.bfloat16)
    residual_wide = lax.optimization_barrier(residual).astype(jnp.float32)
    is_live = jnp.arange(tok_rows, dtype=jnp.int32) < row_counts[0]
    expert_total = lax.axis_size(("ep", "rep")) * w_in.shape[0]
    capacity = min(tok_rows, max(2, 2 * tok_rows * TOPK // expert_total))
    pair_count = tok_rows * TOPK
    flat_ids = route_ids.reshape(pair_count)
    pair_hits = (
        flat_ids[:, None] == jnp.arange(expert_total, dtype=jnp.int32)[None, :]
    ) & jnp.repeat(is_live, TOPK)[:, None]
    hit_counts = pair_hits.astype(jnp.int32)
    earlier_hits = jnp.cumsum(hit_counts, axis=0) - hit_counts
    slot_index = jnp.sum(earlier_hits * hit_counts, axis=1)
    target_cell = jnp.where(
        jnp.any(pair_hits, axis=1), flat_ids * capacity + slot_index, -1
    ).reshape(tok_rows, TOPK)
    cell_index = jnp.arange(expert_total * capacity, dtype=jnp.int32)
    cell_hits = target_cell[None, :, :] == cell_index[:, None, None]
    dispatch_rows = jnp.any(cell_hits, axis=2).astype(jnp.bfloat16)
    combine_rows = jnp.sum(
        jnp.where(cell_hits, route_weight.astype(jnp.float32)[None], 0.0), axis=2
    ).astype(jnp.bfloat16)
    full_rows = lax.all_gather(residual, "seq", axis=1, tiled=True)
    rows_wide = full_rows.astype(jnp.float32)
    inverse_rms = lax.rsqrt(jnp.mean(rows_wide * rows_wide, axis=1) + epsilon)
    normed = (rows_wide * inverse_rms[:, None] * moe_gain).astype(jnp.bfloat16)
    outgoing = jnp.dot(dispatch_rows, normed, preferred_element_type=jnp.float32).astype(
        jnp.bfloat16
    )
    outgoing = outgoing.reshape(expert_total, capacity, D)
    arrived = lax.all_to_all(outgoing, ("ep", "rep"), split_axis=0, concat_axis=0, tiled=True)
    sources, slot_count, feature_count = arrived.shape
    flat_rows = arrived.reshape(sources * slot_count, D)
    gate_up = jnp.dot(flat_rows, w_in.reshape(D, -1), preferred_element_type=jnp.float32).reshape(
        sources * slot_count, 2, -1
    )
    hidden_units = (jax.nn.silu(gate_up[:, 0]) * gate_up[:, 1]).astype(jnp.bfloat16)
    down_part = jnp.dot(
        hidden_units, w_down.reshape(-1, D), preferred_element_type=jnp.float32
    ).reshape(sources, slot_count, D)
    summed = lax.psum_scatter(down_part, "seq", scatter_dimension=2, tiled=True).astype(
        jnp.bfloat16
    )
    returned = lax.all_to_all(summed, ("ep", "rep"), split_axis=0, concat_axis=0, tiled=True)
    returned = returned.reshape(expert_total * capacity, feat_local)
    moe_out = lax.dot_general(
        combine_rows, returned, (((0,), (0,)), ((), ())), preferred_element_type=jnp.float32
    )
    mixed = jnp.where(is_live[:, None], residual_wide + moe_out, 0.0).astype(jnp.bfloat16)
    return mixed


LANES = 128
F32 = jnp.float32
BF16 = jnp.bfloat16


def layer_kernel(
    owners,
    qkv_ref,
    lens_ref,
    kv_hbm,
    w_out_ref,
    hidden_ref,
    gain_ref,
    ids_ref,
    gate_ref,
    count_ref,
    w_in_hbm,
    w_down_hbm,
    out_ref,
    kv_buf,
    q_buf,
    pair_out,
    pair_in,
    col_out,
    col_in,
    total,
    rows_all,
    w_raw,
    w_in_buf,
    w_down_buf,
    hidden_buf,
    y_all,
    y_in,
    kv_sem,
    raw_sem,
    w_sem,
    q_send,
    q_recv,
    f_send,
    f_recv,
    pair_send,
    pair_recv,
    col_send,
    col_recv,
    up_send,
    down_send,
    x_send,
    s_send,
    g_recv,
    y_send,
    y_recv,
    pair_send2,
    pair_recv2,
    col_send2,
    col_recv2,
):
    cols = owners // 2
    me = lax.axis_index("ep")
    rep = lax.axis_index("rep")
    mz, mx = me // 2, me % 2
    across = mz * 2 + (1 - mx)
    sister = 1 - rep
    block, width = hidden_ref.shape
    part = kv_buf.shape[-1]
    positions = kv_buf.shape[-2]
    slots = kv_buf.shape[0]
    heads = part // HEAD_DIM
    used = heads * block
    steps = owners

    def remote(src, dst, send, recv, ep=None, core=None):
        return pltpu.make_async_remote_copy(
            src_ref=src,
            dst_ref=dst,
            send_sem=send,
            recv_sem=recv,
            device_id={"ep": me if ep is None else ep, "rep": rep if core is None else core},
            device_id_type=pl.DeviceIdType.MESH,
        )

    def z_of(j):
        if cols == 4:
            k = 3 - j
            return (mz // 2 + k // 2) % 2 * 2 + (mz + k) % 2
        return (mz + 1 + j) % cols

    def owner_of(s):
        return z_of(s % cols) * 2 + (1 - mx + s // cols) % 2

    def kv_copy(s):
        return pltpu.make_async_copy(
            kv_hbm.at[:, owner_of(s)], kv_buf.at[s % slots], kv_sem.at[s % slots]
        )

    tiles = w_raw.shape[0]

    def raw_copy(n):
        return pltpu.make_async_copy(
            w_in_hbm.at[:, :, pl.ds(n * LANES, LANES)], w_raw.at[n], raw_sem.at[n]
        )

    down_copy = pltpu.make_async_copy(w_down_hbm, w_down_buf, w_sem)
    for s in range(slots):
        kv_copy(s).start()

    barrier = pltpu.get_barrier_semaphore()
    for i in range(1, owners):
        pl.semaphore_signal(
            barrier,
            inc=1,
            device_id={"ep": (me + i) % owners, "rep": rep},
            device_id_type=pl.DeviceIdType.MESH,
        )
    pl.semaphore_signal(
        barrier, inc=1, device_id={"ep": me, "rep": sister}, device_id_type=pl.DeviceIdType.MESH
    )
    pl.semaphore_wait(barrier, owners)

    def lanes_of(owner):
        return pl.ds(pl.multiple_of(owner * part, part), part)

    def q_copy(to, slot):
        return remote(
            qkv_ref.at[pl.ds(0, 1), :, lanes_of(to)],
            q_buf.at[slot, pl.ds(0, 1)],
            q_send.at[to],
            q_recv.at[slot],
            ep=to,
        )

    def f_copy(to, slot):
        return remote(
            qkv_ref.at[pl.ds(1, 2), :, lanes_of(to)],
            q_buf.at[slot, pl.ds(1, 2)],
            f_send.at[to],
            f_recv.at[slot],
            ep=to,
        )

    for s in range(steps - 1):
        q_copy(owner_of(s), me).start()
    for s in range(steps - 1):
        f_copy(owner_of(s), me).start()

    q_buf[me] = qkv_ref[:, :, lanes_of(me)]

    is_live = lax.broadcasted_iota(jnp.int32, (block, 1), 0) < count_ref[0]
    expert_id = lax.broadcasted_iota(jnp.int32, (LANES, LANES), 0)
    gates = gate_ref[...].astype(F32)
    ids = jnp.concatenate([ids_ref[...]] * (LANES // block), axis=1)
    gates = jnp.concatenate([gates] * (LANES // block), axis=1)
    coef = jnp.zeros((LANES, LANES), F32)
    for k in range(TOPK):
        coef += jnp.where(expert_id == ids[k : k + 1], gates[k : k + 1], 0.0)
    coef = coef.T[:block]
    rows_all[mx, rep, mz, :, width:] = jnp.where(is_live, coef, 0.0).astype(BF16)

    lane_row = lax.broadcasted_iota(jnp.int32, (1, LANES), 1) % block
    pos_of = lax.broadcasted_iota(jnp.int32, (positions, LANES), 0)
    head_of = lax.broadcasted_iota(jnp.int32, (block, part), 1) // HEAD_DIM
    row_mod = lax.broadcasted_iota(jnp.int32, (used, positions), 0) % block
    scale = 1.0 / math.sqrt(HEAD_DIM)
    group = 8

    def partial(s):
        owner, slot = owner_of(s), s % slots

        @pl.when(owner != me)
        def _():
            q_copy(owner, owner).wait_recv()

        kv_copy(s).wait()
        query = q_buf[owner, 0]
        zero = jnp.zeros_like(query)
        stack = [jnp.where(head_of == h, query, zero) for h in range(heads)]
        stack += [zero] * (LANES // block - heads)
        queries = jnp.concatenate(stack, axis=0)
        nt = (((1,), (1,)), ((), ()))

        def score_step(g, acc):
            keys = kv_buf[slot, 0, pl.ds(g * group, group)].reshape(group * positions, part)
            got = lax.dot_general(keys, queries, nt, preferred_element_type=F32)
            for r in range(group):
                acc = jnp.where(
                    lane_row == g * group + r, got[r * positions : (r + 1) * positions], acc
                )
            return acc

        scores = lax.fori_loop(
            0, block // group, score_step, jnp.zeros((positions, LANES), F32)
        )

        @pl.when(owner != me)
        def _():
            f_copy(owner, owner).wait_recv()

        fresh_k = q_buf[owner, 1]
        fresh_v = q_buf[owner, 2].astype(F32)
        fresh = lax.dot_general(fresh_k, queries, nt, preferred_element_type=F32)
        diag = lax.broadcasted_iota(jnp.int32, (block, LANES), 0) == (
            lax.broadcasted_iota(jnp.int32, (block, LANES), 1) % block
        )
        own = jnp.sum(jnp.where(diag, fresh, 0.0), axis=0, keepdims=True) * scale
        lens = jnp.concatenate([lens_ref[pl.ds(owner, 1), :]] * (LANES // block), axis=1)
        in_cache = pos_of < lens
        scores = jnp.where(in_cache, scores * scale, masked_score)
        top = jnp.maximum(jnp.max(scores, axis=0, keepdims=True), own)
        weights = jnp.where(in_cache, jnp.exp(scores - top), 0.0)
        own_w = jnp.exp(own - top)
        den = jnp.sum(weights, axis=0, keepdims=True) + own_w
        own_t = jnp.broadcast_to(own_w, (LANES, LANES)).T
        den_t = jnp.broadcast_to(den, (LANES, LANES)).T
        weights_t = weights.T[:used]

        def value_step(g, acc):
            wide = jnp.concatenate(
                [
                    jnp.where(row_mod == g * group + r, weights_t, 0.0).astype(BF16)
                    for r in range(group)
                ],
                axis=1,
            )
            values = kv_buf[slot, 1, pl.ds(g * group, group)].reshape(group * positions, part)
            return acc + jnp.dot(wide, values, preferred_element_type=F32)

        summed = lax.fori_loop(0, block // group, value_step, jnp.zeros((used, part), F32))

        @pl.when(s + slots < steps)
        def _():
            kv_copy(s + slots).start()

        pieces = []
        for h in range(heads):
            rows = slice(h * block, (h + 1) * block)
            lanes = slice(h * HEAD_DIM, (h + 1) * HEAD_DIM)
            pieces.append((summed[rows, lanes] + own_t[rows] * fresh_v[:, lanes]) / den_t[rows])
        attended = jnp.concatenate(pieces, axis=1).astype(BF16)
        return jnp.dot(attended, w_out_ref[...], preferred_element_type=F32)

    def pair_copy(z):
        return remote(pair_out.at[z], pair_in.at[z], pair_send.at[z], pair_recv.at[z], ep=across)

    def col_copy(z, slot):
        return remote(
            col_out.at[z], col_in.at[slot], col_send.at[z], col_recv.at[slot], ep=z * 2 + mx
        )

    @pl.loop(0, cols)
    def _(j):
        z = z_of(j)
        pair_out[z] = partial(j).astype(BF16)
        pair_copy(z).start()

    for n in range(tiles):
        raw_copy(n).start()
    down_copy.start()

    @pl.loop(0, cols)
    def _(j):
        z = z_of(j)
        mine = partial(cols + j)
        pair_copy(z).wait_recv()
        mine = mine + pair_in[z].astype(F32)

        @pl.when(j < cols - 1)
        def _():
            col_out[z] = mine.astype(BF16)
            col_copy(z, mz).start()

        @pl.when(j == cols - 1)
        def _():
            total[...] = mine

    flat = w_raw.reshape(tiles, 2 * width, LANES)
    chunk = 2 * LANES
    pick_row = lax.broadcasted_iota(jnp.int32, (chunk, chunk), 0)
    pick_col = lax.broadcasted_iota(jnp.int32, (chunk, chunk), 1)
    pick = jnp.where(
        pick_col == pick_row % LANES * 2 + pick_row // LANES, 1.0, 0.0
    ).astype(BF16)
    turns = 2 * width // chunk
    unroll = 4

    def planes(low, high):
        @pl.loop(low, high)
        def _(turn):
            for n in range(0, tiles, 2):
                many = min(2, tiles - n)
                for k in range(unroll):
                    i = turn * unroll + k
                    raw_rows = pl.ds(pl.multiple_of(i * chunk, chunk), chunk)
                    out_rows = pl.ds(pl.multiple_of(i * LANES, LANES), LANES)
                    both = jnp.concatenate(
                        [flat[n + t, raw_rows, :] for t in range(many)], axis=1
                    )
                    split = jnp.dot(pick, both, preferred_element_type=F32).astype(BF16)
                    for t in range(many):
                        at = (n + t) * chunk
                        lanes = slice(t * LANES, (t + 1) * LANES)
                        w_in_buf[out_rows, at : at + LANES] = split[:LANES, lanes]
                        w_in_buf[out_rows, at + LANES : at + chunk] = split[LANES:, lanes]

    rounds = turns // unroll
    cuts = [rounds * i // 4 for i in range(5)]
    for n in range(tiles):
        raw_copy(n).wait()
    planes(cuts[0], cuts[1])

    for j in range(cols - 1):
        z = z_of(j)
        col_copy(z, z).wait_recv()
        total[...] += col_in[z].astype(F32)
    residual = (hidden_ref[...].astype(F32) + total[...]).astype(BF16)
    wide = residual.astype(F32)
    total[...] = wide
    inverse = lax.rsqrt(jnp.mean(wide * wide, axis=1, keepdims=True) + epsilon)
    rows_all[mx, rep, mz, :, :width] = (wide * inverse * gain_ref[...]).astype(BF16)

    def row_copy(e, side, send, ep=None, core=None):
        at = rows_all.at[e % 2, side, e // 2]
        return remote(at, at, send, g_recv.at[e % 2, side, e // 2], ep=ep, core=core)

    def up_copy(z):
        return row_copy(z * 2 + mx, rep, up_send.at[z], ep=me + 2)

    def lower_copy(z):
        return row_copy(z * 2 + mx, rep, down_send.at[z], ep=me - 2)

    def x_copy(e):
        return row_copy(e, rep, x_send.at[e], ep=across)

    def s_copy(e, side):
        return row_copy(e, side, s_send.at[e], core=sister)

    def send_up(z):
        @pl.when(mz < cols - 1)
        def _():
            up_copy(z).start()

    def send_down(z):
        @pl.when(mz > 0)
        def _():
            lower_copy(z).start()

    send_up(mz)
    send_down(mz)
    x_copy(me).start()
    s_copy(me, rep).start()
    for d in range(1, cols):
        planes(cuts[min(d, 4)], cuts[min(d + 1, 4)])

        @pl.when(mz - d >= 0)
        def _():
            z = mz - d
            x_copy(z * 2 + mx).wait_recv()
            send_up(z)
            x_copy(z * 2 + mx).start()
            s_copy(z * 2 + mx, rep).start()

        @pl.when(mz + d < cols)
        def _():
            z = mz + d
            x_copy(z * 2 + mx).wait_recv()
            send_down(z)
            x_copy(z * 2 + mx).start()
            s_copy(z * 2 + mx, rep).start()

    for d in range(cols, 4):
        planes(cuts[d], cuts[d + 1])

    expert = me * 2 + rep
    half = owners * block
    step = 2 * LANES

    def gate_up(x, low, high):
        @pl.loop(low, high)
        def _(n):
            rows = rows_all[x, :, :, :, :width].reshape(half, width)
            lanes = pl.ds(pl.multiple_of(n * LANES, LANES), LANES)
            both = jnp.dot(
                rows,
                w_in_buf[:, pl.ds(pl.multiple_of(n * chunk, chunk), chunk)],
                preferred_element_type=F32,
            )
            gate, up = both[:, :LANES], both[:, LANES:]
            hidden_buf[x, :, lanes] = (gate / (1.0 + jnp.exp(-gate)) * up).astype(BF16)

    def down(x):
        coefs = rows_all[x, :, :, :, width:].reshape(half, LANES).astype(F32)
        lane = lax.broadcasted_iota(jnp.int32, (half, LANES), 1)
        factor = jnp.sum(jnp.where(lane == expert, coefs, 0.0), axis=1, keepdims=True)

        @pl.loop(0, width // step)
        def _(n):
            lanes = pl.ds(pl.multiple_of(n * step, step), step)
            made = jnp.dot(hidden_buf[x], w_down_buf[:, lanes], preferred_element_type=F32)
            made = made.astype(BF16).astype(F32) * factor
            y_all[x, :, :, :, lanes] = made.astype(BF16).reshape(2, cols, block, step)

    def y_copy(x, z):
        return remote(
            y_all.at[x, sister, z], y_in.at[x, z], y_send.at[x, z], y_recv.at[x, z], core=sister
        )

    def across_arrive(d):
        @pl.when(mz - d >= 0)
        def _():
            e = (mz - d) * 2 + 1 - mx
            x_copy(e).wait_recv()
            s_copy(e, rep).start()

        if d:

            @pl.when(mz + d < cols)
            def _():
                e = (mz + d) * 2 + 1 - mx
                x_copy(e).wait_recv()
                s_copy(e, rep).start()

    for z in range(cols):
        s_copy(z * 2 + mx, sister).wait_recv()
    gate_up(mx, 0, tiles // 2)
    for d in range(cols - 1):
        across_arrive(d)
    gate_up(mx, tiles // 2, tiles)
    across_arrive(cols - 1)
    down_copy.wait()
    for z in range(cols):
        s_copy(z * 2 + 1 - mx, sister).wait_recv()
    gate_up(1 - mx, 0, tiles)
    down(1 - mx)
    for j in range(cols):
        y_copy(1 - mx, z_of(j)).start()

    def pair_copy2(z):
        return remote(
            pair_out.at[z], pair_in.at[z], pair_send2.at[z], pair_recv2.at[z], ep=across
        )

    def col_copy2(z, slot):
        return remote(
            col_out.at[z], col_in.at[slot], col_send2.at[z], col_recv2.at[slot], ep=z * 2 + mx
        )

    for z in range(cols):
        pair_copy(z).wait_send()
    for j in range(cols - 1):
        col_copy(z_of(j), mz).wait_send()
    for j in range(cols):
        z = z_of(j)
        y_copy(1 - mx, z).wait_recv()
        made = y_all[1 - mx, rep, z].astype(F32) + y_in[1 - mx, z].astype(F32)
        pair_out[z] = made.astype(BF16)
        pair_copy2(z).start()
    down(mx)
    for j in range(cols):
        y_copy(mx, z_of(j)).start()
    for j in range(cols):
        z = z_of(j)
        y_copy(mx, z).wait_recv()
        made = y_all[mx, rep, z].astype(F32) + y_in[mx, z].astype(F32)
        pair_copy2(z).wait_recv()
        mine = made + pair_in[z].astype(F32)
        if j < cols - 1:
            col_out[z] = mine.astype(BF16)
            col_copy2(z, mz).start()
        else:
            total[...] += mine
    for j in range(cols - 1):
        z = z_of(j)
        col_copy2(z, z).wait_recv()
        total[...] += col_in[z].astype(F32)
    out_ref[...] = jnp.where(is_live, total[...], 0.0).astype(BF16)

    for s in range(steps - 1):
        q_copy(owner_of(s), me).wait_send()
        f_copy(owner_of(s), me).wait_send()
    for x in range(2):
        for z in range(cols):
            y_copy(x, z).wait_send()
    for z in range(cols):
        pair_copy2(z).wait_send()
        x_copy(z * 2 + mx).wait_send()
    for j in range(cols - 1):
        col_copy2(z_of(j), mz).wait_send()

    for z in range(cols):

        @pl.when((z <= mz) & (mz < cols - 1))
        def _():
            up_copy(z).wait_send()

        @pl.when((z >= mz) & (mz > 0))
        def _():
            lower_copy(z).wait_send()

    for e in range(owners):
        s_copy(e, rep).wait_send()


def fast_local(
    owners,
    hidden_in,
    row_counts,
    qkv_new,
    cache_len,
    kv_cache,
    w_out,
    moe_gain,
    w_in,
    w_down,
    route_ids,
    route_weight,
):
    block, width = hidden_in.shape
    part = kv_cache.shape[-1]
    positions = kv_cache.shape[3]
    cols = owners // 2
    inner = w_down.shape[1]
    tiles = inner // LANES
    fresh = jnp.transpose(qkv_new, (1, 0, 2))
    vmem = pl.BlockSpec(memory_space=pltpu.VMEM)
    hbm = pl.BlockSpec(memory_space=pl.ANY)
    smem = pl.BlockSpec(memory_space=pltpu.SMEM)
    dma = pltpu.SemaphoreType.DMA
    wide = (cols, block, width)
    slots = min(3, owners)
    return pl.pallas_call(
        functools.partial(layer_kernel, owners),
        out_shape=jax.ShapeDtypeStruct((block, width), BF16),
        in_specs=[vmem, vmem, hbm, vmem, vmem, vmem, vmem, vmem, smem, hbm, hbm],
        out_specs=vmem,
        scratch_shapes=[
            pltpu.VMEM((slots, 2, block, positions, part), BF16),
            pltpu.VMEM((owners, 3, block, part), BF16),
            pltpu.VMEM(wide, BF16),
            pltpu.VMEM(wide, BF16),
            pltpu.VMEM(wide, BF16),
            pltpu.VMEM(wide, BF16),
            pltpu.VMEM((block, width), F32),
            pltpu.VMEM((2, 2, cols, block, width + LANES), BF16),
            pltpu.VMEM((tiles, width, 2, LANES), BF16),
            pltpu.VMEM((width, 2 * inner), BF16),
            pltpu.VMEM((inner, width), BF16),
            pltpu.VMEM((2, owners * block, inner), BF16),
            pltpu.VMEM((2, 2, cols, block, width), BF16),
            pltpu.VMEM((2, cols, block, width), BF16),
            dma((slots,)),
            dma((tiles,)),
            dma,
            dma((owners,)),
            dma((owners,)),
            dma((owners,)),
            dma((owners,)),
            dma((cols,)),
            dma((cols,)),
            dma((cols,)),
            dma((cols,)),
            dma((cols,)),
            dma((cols,)),
            dma((owners,)),
            dma((owners,)),
            dma((2, 2, cols)),
            dma((2, cols)),
            dma((2, cols)),
            dma((cols,)),
            dma((cols,)),
            dma((cols,)),
            dma((cols,)),
        ],
        compiler_params=pltpu.CompilerParams(
            collective_id=0, has_side_effects=True, vmem_limit_bytes=63 * 1024 * 1024
        ),
    )(
        fresh,
        cache_len,
        kv_cache,
        w_out,
        hidden_in,
        moe_gain.reshape(1, width),
        route_ids.T,
        route_weight.T,
        row_counts,
        w_in.reshape(width, 2, inner),
        w_down.reshape(inner, width),
    )


def solution(mesh):
    placed = (
        P(("grp", "ep", "rep"), "seq"),
        P(("grp", "ep", "rep")),
        P(("grp", "ep", "rep"), None, None),
        P("grp", ("rep", "seq")),
        P(None, "grp", ("rep", "seq"), None, "ep"),
        P("ep", "seq"),
        P(),
        P(("ep", "rep"), None, None, "seq"),
        P(("ep", "rep"), "seq", None),
        P(("grp", "ep", "rep"), None),
        P(("grp", "ep", "rep"), None),
    )
    sizes = mesh.shape
    owners = sizes["ep"]
    one_step = sizes["seq"] == 1 and sizes["rep"] == 2 and owners % 2 == 0 and owners <= 8
    body = functools.partial(fast_local, owners) if one_step else local
    return jax.shard_map(
        body, mesh=mesh, in_specs=placed, out_specs=P(("grp", "ep", "rep"), "seq"), check_vma=False
    )
```

```python
import functools
import math

import jax
import jax.numpy as jnp
from jax import lax
from jax.experimental import pallas as pl
from jax.experimental.pallas import tpu as pltpu
from jax.sharding import PartitionSpec as P

D = 2048
HEAD_DIM = 128
TOPK = 6


epsilon = 1e-06
masked_score = -1e30


def local(
    hidden_in,
    row_counts,
    qkv_new,
    cache_len,
    kv_cache,
    w_out,
    moe_gain,
    w_in,
    w_down,
    route_ids,
    route_weight,
):
    tok_rows, feat_local = hidden_in.shape
    owners = lax.axis_size("ep")
    parts_seq = lax.axis_size("seq")
    width_local = kv_cache.shape[-1]
    heads_local = width_local // HEAD_DIM
    positions = kv_cache.shape[3]
    share_rows = tok_rows // parts_seq
    attend_rows = owners * share_rows
    moved_block = lax.all_to_all(qkv_new, "ep", split_axis=2, concat_axis=0, tiled=True)
    moved_block = moved_block.reshape(owners, tok_rows, 3, width_local)
    heads_block = lax.dynamic_slice_in_dim(
        moved_block, lax.axis_index("seq") * share_rows, share_rows, 1
    )
    heads_block = heads_block.reshape(attend_rows, 3, heads_local, HEAD_DIM)
    queries = heads_block[:, 0]
    key_new = heads_block[:, 1].astype(jnp.float32)
    value_new = heads_block[:, 2].astype(jnp.float32)
    lengths = cache_len.reshape(attend_rows)
    cache_keys = kv_cache[0].reshape(attend_rows, positions, heads_local, HEAD_DIM)
    cache_values = kv_cache[1].reshape(attend_rows, positions, heads_local, HEAD_DIM)
    score_scale = 1.0 / math.sqrt(HEAD_DIM)
    position = jnp.arange(positions, dtype=jnp.int32)
    in_cache = position[None, None, :] < lengths[:, None, None]
    scores = (
        jnp.einsum("nhd,nphd->nhp", queries, cache_keys, preferred_element_type=jnp.float32)
        * score_scale
    )
    scores = jnp.where(in_cache, scores, masked_score)
    own_score = jnp.sum(queries.astype(jnp.float32) * key_new, axis=2) * score_scale
    highest = jnp.maximum(jnp.max(scores, axis=2), own_score)
    weights = jnp.where(in_cache, jnp.exp(scores - highest[..., None]), 0.0)
    partial_sum = jnp.einsum(
        "nhp,nphd->nhd",
        weights.astype(jnp.bfloat16),
        cache_values,
        preferred_element_type=jnp.float32,
    )
    own_weight = jnp.exp(own_score - highest)
    attended = (partial_sum + own_weight[..., None] * value_new) / (
        jnp.sum(weights, axis=2) + own_weight
    )[..., None]
    attended = attended.astype(jnp.bfloat16).reshape(owners, share_rows, width_local)
    attended = lax.all_gather(attended, "seq", axis=1, tiled=True).reshape(
        owners * tok_rows, width_local
    )
    attn_out = lax.psum_scatter(
        jnp.dot(attended, w_out, preferred_element_type=jnp.float32),
        "ep",
        scatter_dimension=0,
        tiled=True,
    )
    residual = (hidden_in.astype(jnp.float32) + attn_out).astype(jnp.bfloat16)
    residual_wide = lax.optimization_barrier(residual).astype(jnp.float32)
    is_live = jnp.arange(tok_rows, dtype=jnp.int32) < row_counts[0]
    expert_total = lax.axis_size(("ep", "rep")) * w_in.shape[0]
    capacity = min(tok_rows, max(2, 2 * tok_rows * TOPK // expert_total))
    pair_count = tok_rows * TOPK
    flat_ids = route_ids.reshape(pair_count)
    pair_hits = (
        flat_ids[:, None] == jnp.arange(expert_total, dtype=jnp.int32)[None, :]
    ) & jnp.repeat(is_live, TOPK)[:, None]
    hit_counts = pair_hits.astype(jnp.int32)
    earlier_hits = jnp.cumsum(hit_counts, axis=0) - hit_counts
    slot_index = jnp.sum(earlier_hits * hit_counts, axis=1)
    target_cell = jnp.where(
        jnp.any(pair_hits, axis=1), flat_ids * capacity + slot_index, -1
    ).reshape(tok_rows, TOPK)
    cell_index = jnp.arange(expert_total * capacity, dtype=jnp.int32)
    cell_hits = target_cell[None, :, :] == cell_index[:, None, None]
    dispatch_rows = jnp.any(cell_hits, axis=2).astype(jnp.bfloat16)
    combine_rows = jnp.sum(
        jnp.where(cell_hits, route_weight.astype(jnp.float32)[None], 0.0), axis=2
    ).astype(jnp.bfloat16)
    full_rows = lax.all_gather(residual, "seq", axis=1, tiled=True)
    rows_wide = full_rows.astype(jnp.float32)
    inverse_rms = lax.rsqrt(jnp.mean(rows_wide * rows_wide, axis=1) + epsilon)
    normed = (rows_wide * inverse_rms[:, None] * moe_gain).astype(jnp.bfloat16)
    outgoing = jnp.dot(dispatch_rows, normed, preferred_element_type=jnp.float32).astype(
        jnp.bfloat16
    )
    outgoing = outgoing.reshape(expert_total, capacity, D)
    arrived = lax.all_to_all(outgoing, ("ep", "rep"), split_axis=0, concat_axis=0, tiled=True)
    sources, slot_count, feature_count = arrived.shape
    flat_rows = arrived.reshape(sources * slot_count, D)
    gate_up = jnp.dot(flat_rows, w_in.reshape(D, -1), preferred_element_type=jnp.float32).reshape(
        sources * slot_count, 2, -1
    )
    hidden_units = (jax.nn.silu(gate_up[:, 0]) * gate_up[:, 1]).astype(jnp.bfloat16)
    down_part = jnp.dot(
        hidden_units, w_down.reshape(-1, D), preferred_element_type=jnp.float32
    ).reshape(sources, slot_count, D)
    summed = lax.psum_scatter(down_part, "seq", scatter_dimension=2, tiled=True).astype(
        jnp.bfloat16
    )
    returned = lax.all_to_all(summed, ("ep", "rep"), split_axis=0, concat_axis=0, tiled=True)
    returned = returned.reshape(expert_total * capacity, feat_local)
    moe_out = lax.dot_general(
        combine_rows, returned, (((0,), (0,)), ((), ())), preferred_element_type=jnp.float32
    )
    mixed = jnp.where(is_live[:, None], residual_wide + moe_out, 0.0).astype(jnp.bfloat16)
    return mixed


LANES = 128
F32 = jnp.float32
BF16 = jnp.bfloat16


def layer_kernel(
    owners,
    qkv_ref,
    lens_ref,
    kv_hbm,
    w_out_ref,
    hidden_ref,
    gain_ref,
    ids_ref,
    gate_ref,
    count_ref,
    w_in_hbm,
    w_down_hbm,
    out_ref,
    kv_buf,
    q_buf,
    own_out,
    own_in,
    pair_out,
    pair_in,
    col_out,
    col_in,
    total,
    rows_all,
    w_raw,
    w_in_buf,
    w_down_buf,
    hidden_buf,
    y_all,
    y_in,
    kv_sem,
    raw_sem,
    w_sem,
    q_send,
    q_recv,
    v_send,
    v_recv,
    own_send,
    own_recv,
    pair_send,
    pair_recv,
    col_send,
    col_recv,
    up_send,
    down_send,
    x_send,
    s_send,
    g_recv,
    y_send,
    y_recv,
    pair_send2,
    pair_recv2,
    col_send2,
    col_recv2,
):
    cols = owners // 2
    me = lax.axis_index("ep")
    rep = lax.axis_index("rep")
    mz, mx = me // 2, me % 2
    across = mz * 2 + (1 - mx)
    sister = 1 - rep
    block, width = hidden_ref.shape
    part = kv_buf.shape[-1]
    positions = kv_buf.shape[-2]
    slots = kv_buf.shape[0]
    heads = part // HEAD_DIM
    used = heads * block
    steps = owners

    def remote(src, dst, send, recv, ep=None, core=None):
        return pltpu.make_async_remote_copy(
            src_ref=src,
            dst_ref=dst,
            send_sem=send,
            recv_sem=recv,
            device_id={"ep": me if ep is None else ep, "rep": rep if core is None else core},
            device_id_type=pl.DeviceIdType.MESH,
        )

    def z_of(j):
        if cols == 4:
            k = 3 - j
            return (mz // 2 + k // 2) % 2 * 2 + (mz + k) % 2
        return (mz + 1 + j) % cols

    def second(s):
        t = (s + steps - 1) % steps
        return (1 - t % 2) * ((t + steps - 1) // steps) + t // (steps - 1)

    def turn_of(s):
        return ((s + steps - 1) % steps + 1) // 2 - second(s)

    def owner_of(s):
        return z_of(turn_of(s)) * 2 + (1 - mx + second(s)) % 2

    def kv_copy(s):
        return pltpu.make_async_copy(
            kv_hbm.at[:, owner_of(s)], kv_buf.at[s % slots], kv_sem.at[s % slots]
        )

    tiles = w_raw.shape[0]

    def raw_copy(n):
        return pltpu.make_async_copy(
            w_in_hbm.at[:, :, pl.ds(n * LANES, LANES)], w_raw.at[n], raw_sem.at[n]
        )

    down_copy = pltpu.make_async_copy(w_down_hbm, w_down_buf, w_sem)
    for s in range(slots):
        kv_copy(s).start()

    barrier = pltpu.get_barrier_semaphore()
    for i in range(1, owners):
        pl.semaphore_signal(
            barrier,
            inc=1,
            device_id={"ep": (me + i) % owners, "rep": rep},
            device_id_type=pl.DeviceIdType.MESH,
        )
    pl.semaphore_signal(
        barrier, inc=1, device_id={"ep": me, "rep": sister}, device_id_type=pl.DeviceIdType.MESH
    )
    pl.semaphore_wait(barrier, owners)

    def lanes_of(owner):
        return pl.ds(pl.multiple_of(owner * part, part), part)

    def q_copy(to, slot):
        return remote(
            qkv_ref.at[pl.ds(0, 1), :, lanes_of(to)],
            q_buf.at[slot, pl.ds(0, 1)],
            q_send.at[to],
            q_recv.at[slot],
            ep=to,
        )

    def v_copy(to, slot):
        return remote(
            qkv_ref.at[pl.ds(2, 1), :, lanes_of(to)],
            q_buf.at[slot, pl.ds(1, 1)],
            v_send.at[to],
            v_recv.at[slot],
            ep=to,
        )

    def own_copy(to, slot):
        return remote(
            own_out.at[to], own_in.at[slot], own_send.at[to], own_recv.at[slot], ep=to
        )

    for s in range(1, steps):
        q_copy(owner_of(s), me).start()
    for s in range(1, steps):
        v_copy(owner_of(s), me).start()

    head_of = lax.broadcasted_iota(jnp.int32, (block, part), 1) // HEAD_DIM
    scale = 1.0 / math.sqrt(HEAD_DIM)
    nt = (((1,), (1,)), ((), ()))
    diag = lax.broadcasted_iota(jnp.int32, (block, LANES), 0) == (
        lax.broadcasted_iota(jnp.int32, (block, LANES), 1) % block
    )

    def stacked(query):
        zero = jnp.zeros_like(query)
        stack = [jnp.where(head_of == h, query, zero) for h in range(heads)]
        stack += [zero] * (LANES // block - heads)
        return jnp.concatenate(stack, axis=0)

    for i in range(owners):
        lanes = slice(i * part, (i + 1) * part)
        fresh = lax.dot_general(
            qkv_ref[1, :, lanes], stacked(qkv_ref[0, :, lanes]), nt, preferred_element_type=F32
        )
        own = jnp.sum(jnp.where(diag, fresh, 0.0), axis=0, keepdims=True) * scale
        own_out[i] = jnp.broadcast_to(own, own_out.shape[1:])
    for s in range(1, steps):
        own_copy(owner_of(s), me).start()
    own_in[me] = own_out[me]
    q_buf[me, 0] = qkv_ref[0, :, lanes_of(me)]
    q_buf[me, 1] = qkv_ref[2, :, lanes_of(me)]

    flat = w_raw.reshape(tiles, 2 * width, LANES)
    chunk = 2 * LANES
    pick_row = lax.broadcasted_iota(jnp.int32, (chunk, chunk), 0)
    pick_col = lax.broadcasted_iota(jnp.int32, (chunk, chunk), 1)
    pick = jnp.where(
        pick_col == pick_row % LANES * 2 + pick_row // LANES, 1.0, 0.0
    ).astype(BF16)
    turns = 2 * width // chunk
    unroll = 4

    def planes(low, high):
        @pl.loop(low, high)
        def _(turn):
            for n in range(0, tiles, 2):
                many = min(2, tiles - n)
                for k in range(unroll):
                    i = turn * unroll + k
                    raw_rows = pl.ds(pl.multiple_of(i * chunk, chunk), chunk)
                    out_rows = pl.ds(pl.multiple_of(i * LANES, LANES), LANES)
                    both = jnp.concatenate(
                        [flat[n + t, raw_rows, :] for t in range(many)], axis=1
                    )
                    split = jnp.dot(pick, both, preferred_element_type=F32).astype(BF16)
                    for t in range(many):
                        at = (n + t) * chunk
                        lanes = slice(t * LANES, (t + 1) * LANES)
                        w_in_buf[out_rows, at : at + LANES] = split[:LANES, lanes]
                        w_in_buf[out_rows, at + LANES : at + chunk] = split[LANES:, lanes]

    rounds = turns // unroll
    first, early = 0, rounds // 2

    is_live = lax.broadcasted_iota(jnp.int32, (block, 1), 0) < count_ref[0]
    expert_id = lax.broadcasted_iota(jnp.int32, (LANES, LANES), 0)
    gates = gate_ref[...].astype(F32)
    ids = jnp.concatenate([ids_ref[...]] * (LANES // block), axis=1)
    gates = jnp.concatenate([gates] * (LANES // block), axis=1)
    coef = jnp.zeros((LANES, LANES), F32)
    for k in range(TOPK):
        coef += jnp.where(expert_id == ids[k : k + 1], gates[k : k + 1], 0.0)
    coef = coef.T[:block]
    rows_all[mx, rep, mz, :, width:] = jnp.where(is_live, coef, 0.0).astype(BF16)

    lane_row = lax.broadcasted_iota(jnp.int32, (1, LANES), 1) % block
    pos_of = lax.broadcasted_iota(jnp.int32, (positions, LANES), 0)
    row_mod = lax.broadcasted_iota(jnp.int32, (used, positions), 0) % block
    group = 8

    def partial(s):
        owner, slot = owner_of(s), s % slots

        @pl.when(owner != me)
        def _():
            q_copy(owner, owner).wait_recv()

        kv_copy(s).wait()
        queries = stacked(q_buf[owner, 0])

        scores = jnp.zeros((positions, LANES), F32)
        for g in range(block // group):
            keys = kv_buf[slot, 0, g * group : (g + 1) * group].reshape(group * positions, part)
            got = lax.dot_general(keys, queries, nt, preferred_element_type=F32)
            for r in range(group):
                scores = jnp.where(
                    lane_row == g * group + r, got[r * positions : (r + 1) * positions], scores
                )

        @pl.when(owner != me)
        def _():
            own_copy(owner, owner).wait_recv()

        own = own_in[owner][:1]
        lens = jnp.concatenate([lens_ref[pl.ds(owner, 1), :]] * (LANES // block), axis=1)
        in_cache = pos_of < lens
        scores = jnp.where(in_cache, scores * scale, masked_score)
        top = jnp.maximum(jnp.max(scores, axis=0, keepdims=True), own)
        weights = jnp.where(in_cache, jnp.exp(scores - top), 0.0)
        own_w = jnp.exp(own - top)
        den = jnp.sum(weights, axis=0, keepdims=True) + own_w
        own_t = jnp.broadcast_to(own_w, (LANES, LANES)).T
        den_t = jnp.broadcast_to(den, (LANES, LANES)).T
        weights_t = weights.T[:used]

        summed = jnp.zeros((used, part), F32)
        for g in range(block // group):
            wide = jnp.concatenate(
                [
                    jnp.where(row_mod == g * group + r, weights_t, 0.0).astype(BF16)
                    for r in range(group)
                ],
                axis=1,
            )
            values = kv_buf[slot, 1, g * group : (g + 1) * group].reshape(group * positions, part)
            summed += jnp.dot(wide, values, preferred_element_type=F32)

        @pl.when(s + slots < steps)
        def _():
            kv_copy(s + slots).start()

        @pl.when(owner != me)
        def _():
            v_copy(owner, owner).wait_recv()

        fresh_v = q_buf[owner, 1].astype(F32)
        pieces = []
        for h in range(heads):
            rows = slice(h * block, (h + 1) * block)
            lanes = slice(h * HEAD_DIM, (h + 1) * HEAD_DIM)
            pieces.append((summed[rows, lanes] + own_t[rows] * fresh_v[:, lanes]) / den_t[rows])
        attended = jnp.concatenate(pieces, axis=1).astype(BF16)
        return jnp.dot(attended, w_out_ref[...], preferred_element_type=F32)

    def pair_copy(z):
        return remote(pair_out.at[z], pair_in.at[z], pair_send.at[z], pair_recv.at[z], ep=across)

    def col_copy(z, slot):
        return remote(
            col_out.at[z], col_in.at[slot], col_send.at[z], col_recv.at[slot], ep=z * 2 + mx
        )

    @pl.loop(0, steps)
    def _(s):
        j = turn_of(s)
        z = z_of(j)
        made = partial(s)

        @pl.when(second(s) == 0)
        def _():
            pair_out[z] = made.astype(BF16)
            pair_copy(z).start()

        @pl.when(s == 1)
        def _():
            for n in range(tiles):
                raw_copy(n).start()

        @pl.when(s == steps - 1)
        def _():
            down_copy.start()

        @pl.when((second(s) == 1) & (s > 0))
        def _():
            pair_copy(z).wait_recv()
            col_out[z] = (made + pair_in[z].astype(F32)).astype(BF16)
            col_copy(z, mz).start()

        @pl.when(s == 0)
        def _():
            total[...] = made

    for n in range(tiles):
        raw_copy(n).wait()
    planes(first, early)
    pair_copy(mz).wait_recv()
    total[...] += pair_in[mz].astype(F32)

    for j in range(cols - 1):
        z = z_of(j)
        col_copy(z, z).wait_recv()
        total[...] += col_in[z].astype(F32)
    residual = (hidden_ref[...].astype(F32) + total[...]).astype(BF16)
    wide = residual.astype(F32)
    total[...] = wide
    inverse = lax.rsqrt(jnp.mean(wide * wide, axis=1, keepdims=True) + epsilon)
    rows_all[mx, rep, mz, :, :width] = (wide * inverse * gain_ref[...]).astype(BF16)

    cut = g_recv.shape[-1]
    bit = block // cut

    def row_copy(e, side, h, send, ep=None, core=None):
        at = rows_all.at[e % 2, side, e // 2, pl.ds(h * bit, bit)]
        return remote(at, at, send, g_recv.at[e % 2, side, e // 2, h], ep=ep, core=core)

    def up_copy(z, h):
        return row_copy(z * 2 + mx, rep, h, up_send.at[z, h], ep=me + 2)

    def lower_copy(z, h):
        return row_copy(z * 2 + mx, rep, h, down_send.at[z, h], ep=me - 2)

    def x_copy(e, h):
        return row_copy(e, rep, h, x_send.at[e, h], ep=across)

    def s_copy(e, side, h):
        return row_copy(e, side, h, s_send.at[e, h], core=sister)

    def send_up(z, h):
        @pl.when(mz < cols - 1)
        def _():
            up_copy(z, h).start()

    def send_down(z, h):
        @pl.when(mz > 0)
        def _():
            lower_copy(z, h).start()

    for h in range(cut):
        send_up(mz, h)
        send_down(mz, h)
        x_copy(me, h).start()
        s_copy(me, rep, h).start()
    planes(early, rounds * 3 // 4)
    for d in range(1, cols):
        if d == min(2, cols - 1):
            planes(rounds * 3 // 4, rounds)
        for h in range(cut):

            @pl.when(mz - d >= 0)
            def _():
                z = mz - d
                x_copy(z * 2 + mx, h).wait_recv()
                send_up(z, h)
                x_copy(z * 2 + mx, h).start()
                s_copy(z * 2 + mx, rep, h).start()

            @pl.when(mz + d < cols)
            def _():
                z = mz + d
                x_copy(z * 2 + mx, h).wait_recv()
                send_down(z, h)
                x_copy(z * 2 + mx, h).start()
                s_copy(z * 2 + mx, rep, h).start()

    expert = me * 2 + rep
    half = owners * block
    step = 4 * LANES

    def gate_up(x, low, high):
        def some(at, many):
            rows = rows_all[x, :, :, :, :width].reshape(half, width)
            both = jnp.dot(
                rows,
                w_in_buf[:, pl.ds(pl.multiple_of(at * chunk, chunk), many * chunk)],
                preferred_element_type=F32,
            )
            for t in range(many):
                gate = both[:, t * chunk : t * chunk + LANES]
                up = both[:, t * chunk + LANES : (t + 1) * chunk]
                lanes = pl.ds(pl.multiple_of((at + t) * LANES, LANES), LANES)
                hidden_buf[x, :, lanes] = (gate / (1.0 + jnp.exp(-gate)) * up).astype(BF16)

        pairs = (high - low) // 2

        @pl.loop(0, pairs)
        def _(n):
            some(low + 2 * n, 2)

        if low + 2 * pairs < high:
            some(high - 1, 1)

    def down(x):
        coefs = rows_all[x, :, :, :, width:].reshape(half, LANES).astype(F32)
        lane = lax.broadcasted_iota(jnp.int32, (half, LANES), 1)
        factor = jnp.sum(jnp.where(lane == expert, coefs, 0.0), axis=1, keepdims=True)

        @pl.loop(0, width // step)
        def _(n):
            lanes = pl.ds(pl.multiple_of(n * step, step), step)
            made = jnp.dot(hidden_buf[x], w_down_buf[:, lanes], preferred_element_type=F32)
            made = made.astype(BF16).astype(F32) * factor
            y_all[x, :, :, :, lanes] = made.astype(BF16).reshape(2, cols, block, step)

    def y_copy(x, z):
        return remote(
            y_all.at[x, sister, z], y_in.at[x, z], y_send.at[x, z], y_recv.at[x, z], core=sister
        )

    def across_arrive(d):
        for h in range(cut):

            @pl.when(mz - d >= 0)
            def _():
                e = (mz - d) * 2 + 1 - mx
                x_copy(e, h).wait_recv()
                s_copy(e, rep, h).start()

            if d:

                @pl.when(mz + d < cols)
                def _():
                    e = (mz + d) * 2 + 1 - mx
                    x_copy(e, h).wait_recv()
                    s_copy(e, rep, h).start()

    def sister_arrive(x):
        for z in range(cols):
            for h in range(cut):
                s_copy(z * 2 + x, sister, h).wait_recv()

    sister_arrive(mx)
    gate_up(mx, 0, tiles // 4 * 2)
    for d in range(cols - 1):
        across_arrive(d)
    gate_up(mx, tiles // 4 * 2, tiles)
    across_arrive(cols - 1)
    down_copy.wait()
    sister_arrive(1 - mx)
    gate_up(1 - mx, 0, tiles)
    down(1 - mx)
    for j in range(cols):
        y_copy(1 - mx, z_of(j)).start()

    def pair_copy2(z):
        return remote(
            pair_out.at[z], pair_in.at[z], pair_send2.at[z], pair_recv2.at[z], ep=across
        )

    def col_copy2(z, slot):
        return remote(
            col_out.at[z], col_in.at[slot], col_send2.at[z], col_recv2.at[slot], ep=z * 2 + mx
        )

    for z in range(cols):
        pair_copy(z).wait_send()
    for j in range(cols - 1):
        col_copy(z_of(j), mz).wait_send()
    for j in range(cols):
        z = z_of(j)
        y_copy(1 - mx, z).wait_recv()
        made = y_all[1 - mx, rep, z].astype(F32) + y_in[1 - mx, z].astype(F32)
        pair_out[z] = made.astype(BF16)
        pair_copy2(z).start()
    down(mx)
    for j in range(cols):
        y_copy(mx, z_of(j)).start()
    for j in range(cols):
        z = z_of(j)
        y_copy(mx, z).wait_recv()
        made = y_all[mx, rep, z].astype(F32) + y_in[mx, z].astype(F32)
        pair_copy2(z).wait_recv()
        mine = made + pair_in[z].astype(F32)
        if j < cols - 1:
            col_out[z] = mine.astype(BF16)
            col_copy2(z, mz).start()
        else:
            total[...] += mine
    for j in range(cols - 1):
        z = z_of(j)
        col_copy2(z, z).wait_recv()
        total[...] += col_in[z].astype(F32)
    out_ref[...] = jnp.where(is_live, total[...], 0.0).astype(BF16)

    for s in range(1, steps):
        q_copy(owner_of(s), me).wait_send()
        v_copy(owner_of(s), me).wait_send()
        own_copy(owner_of(s), me).wait_send()
    for x in range(2):
        for z in range(cols):
            y_copy(x, z).wait_send()
    for z in range(cols):
        pair_copy2(z).wait_send()
        for h in range(cut):
            x_copy(z * 2 + mx, h).wait_send()
    for j in range(cols - 1):
        col_copy2(z_of(j), mz).wait_send()

    for z in range(cols):

        @pl.when((z <= mz) & (mz < cols - 1))
        def _():
            for h in range(cut):
                up_copy(z, h).wait_send()

        @pl.when((z >= mz) & (mz > 0))
        def _():
            for h in range(cut):
                lower_copy(z, h).wait_send()

    for e in range(owners):
        for h in range(cut):
            s_copy(e, rep, h).wait_send()


def fast_local(
    owners,
    hidden_in,
    row_counts,
    qkv_new,
    cache_len,
    kv_cache,
    w_out,
    moe_gain,
    w_in,
    w_down,
    route_ids,
    route_weight,
):
    block, width = hidden_in.shape
    part = kv_cache.shape[-1]
    positions = kv_cache.shape[3]
    cols = owners // 2
    inner = w_down.shape[1]
    tiles = inner // LANES
    fresh = jnp.transpose(qkv_new, (1, 0, 2))
    vmem = pl.BlockSpec(memory_space=pltpu.VMEM)
    hbm = pl.BlockSpec(memory_space=pl.ANY)
    smem = pl.BlockSpec(memory_space=pltpu.SMEM)
    dma = pltpu.SemaphoreType.DMA
    wide = (cols, block, width)
    slots = min(3, owners)
    cut = 2
    return pl.pallas_call(
        functools.partial(layer_kernel, owners),
        out_shape=jax.ShapeDtypeStruct((block, width), BF16),
        in_specs=[vmem, vmem, hbm, vmem, vmem, vmem, vmem, vmem, smem, hbm, hbm],
        out_specs=vmem,
        scratch_shapes=[
            pltpu.VMEM((slots, 2, block, positions, part), BF16),
            pltpu.VMEM((owners, 2, block, part), BF16),
            pltpu.VMEM((owners, 8, LANES), F32),
            pltpu.VMEM((owners, 8, LANES), F32),
            pltpu.VMEM(wide, BF16),
            pltpu.VMEM(wide, BF16),
            pltpu.VMEM(wide, BF16),
            pltpu.VMEM(wide, BF16),
            pltpu.VMEM((block, width), F32),
            pltpu.VMEM((2, 2, cols, block, width + LANES), BF16),
            pltpu.VMEM((tiles, width, 2, LANES), BF16),
            pltpu.VMEM((width, 2 * inner), BF16),
            pltpu.VMEM((inner, width), BF16),
            pltpu.VMEM((2, owners * block, inner), BF16),
            pltpu.VMEM((2, 2, cols, block, width), BF16),
            pltpu.VMEM((2, cols, block, width), BF16),
            dma((slots,)),
            dma((tiles,)),
            dma,
            dma((owners,)),
            dma((owners,)),
            dma((owners,)),
            dma((owners,)),
            dma((owners,)),
            dma((owners,)),
            dma((cols,)),
            dma((cols,)),
            dma((cols,)),
            dma((cols,)),
            dma((cols, cut)),
            dma((cols, cut)),
            dma((owners, cut)),
            dma((owners, cut)),
            dma((2, 2, cols, cut)),
            dma((2, cols)),
            dma((2, cols)),
            dma((cols,)),
            dma((cols,)),
            dma((cols,)),
            dma((cols,)),
        ],
        compiler_params=pltpu.CompilerParams(
            collective_id=0, has_side_effects=True, vmem_limit_bytes=63 * 1024 * 1024
        ),
    )(
        fresh,
        cache_len,
        kv_cache,
        w_out,
        hidden_in,
        moe_gain.reshape(1, width),
        route_ids.T,
        route_weight.T,
        row_counts,
        w_in.reshape(width, 2, inner),
        w_down.reshape(inner, width),
    )


def solution(mesh):
    placed = (
        P(("grp", "ep", "rep"), "seq"),
        P(("grp", "ep", "rep")),
        P(("grp", "ep", "rep"), None, None),
        P("grp", ("rep", "seq")),
        P(None, "grp", ("rep", "seq"), None, "ep"),
        P("ep", "seq"),
        P(),
        P(("ep", "rep"), None, None, "seq"),
        P(("ep", "rep"), "seq", None),
        P(("grp", "ep", "rep"), None),
        P(("grp", "ep", "rep"), None),
    )
    sizes = mesh.shape
    owners = sizes["ep"]
    one_step = sizes["seq"] == 1 and sizes["rep"] == 2 and owners in (4, 8)
    body = functools.partial(fast_local, owners) if one_step else local
    return jax.shard_map(
        body, mesh=mesh, in_specs=placed, out_specs=P(("grp", "ep", "rep"), "seq"), check_vma=False
    )
```

```python
import functools
import math

import jax
import jax.numpy as jnp
from jax import lax
from jax.experimental import pallas as pl
from jax.experimental.pallas import tpu as pltpu
from jax.sharding import PartitionSpec as P

D = 2048
HEAD_DIM = 128
TOPK = 6


epsilon = 1e-06
masked_score = -1e30


def local(
    hidden_in,
    row_counts,
    qkv_new,
    cache_len,
    kv_cache,
    w_out,
    moe_gain,
    w_in,
    w_down,
    route_ids,
    route_weight,
):
    tok_rows, feat_local = hidden_in.shape
    owners = lax.axis_size("ep")
    parts_seq = lax.axis_size("seq")
    width_local = kv_cache.shape[-1]
    heads_local = width_local // HEAD_DIM
    positions = kv_cache.shape[3]
    share_rows = tok_rows // parts_seq
    attend_rows = owners * share_rows
    moved_block = lax.all_to_all(qkv_new, "ep", split_axis=2, concat_axis=0, tiled=True)
    moved_block = moved_block.reshape(owners, tok_rows, 3, width_local)
    heads_block = lax.dynamic_slice_in_dim(
        moved_block, lax.axis_index("seq") * share_rows, share_rows, 1
    )
    heads_block = heads_block.reshape(attend_rows, 3, heads_local, HEAD_DIM)
    queries = heads_block[:, 0]
    key_new = heads_block[:, 1].astype(jnp.float32)
    value_new = heads_block[:, 2].astype(jnp.float32)
    lengths = cache_len.reshape(attend_rows)
    cache_keys = kv_cache[0].reshape(attend_rows, positions, heads_local, HEAD_DIM)
    cache_values = kv_cache[1].reshape(attend_rows, positions, heads_local, HEAD_DIM)
    score_scale = 1.0 / math.sqrt(HEAD_DIM)
    position = jnp.arange(positions, dtype=jnp.int32)
    in_cache = position[None, None, :] < lengths[:, None, None]
    scores = (
        jnp.einsum("nhd,nphd->nhp", queries, cache_keys, preferred_element_type=jnp.float32)
        * score_scale
    )
    scores = jnp.where(in_cache, scores, masked_score)
    own_score = jnp.sum(queries.astype(jnp.float32) * key_new, axis=2) * score_scale
    highest = jnp.maximum(jnp.max(scores, axis=2), own_score)
    weights = jnp.where(in_cache, jnp.exp(scores - highest[..., None]), 0.0)
    partial_sum = jnp.einsum(
        "nhp,nphd->nhd",
        weights.astype(jnp.bfloat16),
        cache_values,
        preferred_element_type=jnp.float32,
    )
    own_weight = jnp.exp(own_score - highest)
    attended = (partial_sum + own_weight[..., None] * value_new) / (
        jnp.sum(weights, axis=2) + own_weight
    )[..., None]
    attended = attended.astype(jnp.bfloat16).reshape(owners, share_rows, width_local)
    attended = lax.all_gather(attended, "seq", axis=1, tiled=True).reshape(
        owners * tok_rows, width_local
    )
    attn_out = lax.psum_scatter(
        jnp.dot(attended, w_out, preferred_element_type=jnp.float32),
        "ep",
        scatter_dimension=0,
        tiled=True,
    )
    residual = (hidden_in.astype(jnp.float32) + attn_out).astype(jnp.bfloat16)
    residual_wide = lax.optimization_barrier(residual).astype(jnp.float32)
    is_live = jnp.arange(tok_rows, dtype=jnp.int32) < row_counts[0]
    expert_total = lax.axis_size(("ep", "rep")) * w_in.shape[0]
    capacity = min(tok_rows, max(2, 2 * tok_rows * TOPK // expert_total))
    pair_count = tok_rows * TOPK
    flat_ids = route_ids.reshape(pair_count)
    pair_hits = (
        flat_ids[:, None] == jnp.arange(expert_total, dtype=jnp.int32)[None, :]
    ) & jnp.repeat(is_live, TOPK)[:, None]
    hit_counts = pair_hits.astype(jnp.int32)
    earlier_hits = jnp.cumsum(hit_counts, axis=0) - hit_counts
    slot_index = jnp.sum(earlier_hits * hit_counts, axis=1)
    target_cell = jnp.where(
        jnp.any(pair_hits, axis=1), flat_ids * capacity + slot_index, -1
    ).reshape(tok_rows, TOPK)
    cell_index = jnp.arange(expert_total * capacity, dtype=jnp.int32)
    cell_hits = target_cell[None, :, :] == cell_index[:, None, None]
    dispatch_rows = jnp.any(cell_hits, axis=2).astype(jnp.bfloat16)
    combine_rows = jnp.sum(
        jnp.where(cell_hits, route_weight.astype(jnp.float32)[None], 0.0), axis=2
    ).astype(jnp.bfloat16)
    full_rows = lax.all_gather(residual, "seq", axis=1, tiled=True)
    rows_wide = full_rows.astype(jnp.float32)
    inverse_rms = lax.rsqrt(jnp.mean(rows_wide * rows_wide, axis=1) + epsilon)
    normed = (rows_wide * inverse_rms[:, None] * moe_gain).astype(jnp.bfloat16)
    outgoing = jnp.dot(dispatch_rows, normed, preferred_element_type=jnp.float32).astype(
        jnp.bfloat16
    )
    outgoing = outgoing.reshape(expert_total, capacity, D)
    arrived = lax.all_to_all(outgoing, ("ep", "rep"), split_axis=0, concat_axis=0, tiled=True)
    sources, slot_count, feature_count = arrived.shape
    flat_rows = arrived.reshape(sources * slot_count, D)
    gate_up = jnp.dot(flat_rows, w_in.reshape(D, -1), preferred_element_type=jnp.float32).reshape(
        sources * slot_count, 2, -1
    )
    hidden_units = (jax.nn.silu(gate_up[:, 0]) * gate_up[:, 1]).astype(jnp.bfloat16)
    down_part = jnp.dot(
        hidden_units, w_down.reshape(-1, D), preferred_element_type=jnp.float32
    ).reshape(sources, slot_count, D)
    summed = lax.psum_scatter(down_part, "seq", scatter_dimension=2, tiled=True).astype(
        jnp.bfloat16
    )
    returned = lax.all_to_all(summed, ("ep", "rep"), split_axis=0, concat_axis=0, tiled=True)
    returned = returned.reshape(expert_total * capacity, feat_local)
    moe_out = lax.dot_general(
        combine_rows, returned, (((0,), (0,)), ((), ())), preferred_element_type=jnp.float32
    )
    mixed = jnp.where(is_live[:, None], residual_wide + moe_out, 0.0).astype(jnp.bfloat16)
    return mixed


LANES = 128
F32 = jnp.float32
BF16 = jnp.bfloat16


def layer_kernel(
    owners,
    qkv_ref,
    lens_ref,
    kv_hbm,
    w_out_ref,
    hidden_ref,
    gain_ref,
    ids_ref,
    gate_ref,
    count_ref,
    w_in_hbm,
    w_down_hbm,
    out_ref,
    kv_buf,
    q_buf,
    own_out,
    own_in,
    pair_out,
    pair_in,
    col_out,
    col_in,
    total,
    rows_all,
    w_raw,
    w_in_buf,
    w_down_buf,
    hidden_buf,
    y_all,
    y_in,
    kv_sem,
    raw_sem,
    w_sem,
    q_send,
    q_recv,
    v_send,
    v_recv,
    own_send,
    own_recv,
    pair_send,
    pair_recv,
    col_send,
    col_recv,
    up_send,
    down_send,
    x_send,
    s_send,
    g_recv,
    y_send,
    y_recv,
    pair_send2,
    pair_recv2,
    col_send2,
    col_recv2,
):
    cols = owners // 2
    me = lax.axis_index("ep")
    rep = lax.axis_index("rep")
    mz, mx = me // 2, me % 2
    across = mz * 2 + (1 - mx)
    sister = 1 - rep
    block, width = hidden_ref.shape
    part = kv_buf.shape[-1]
    positions = kv_buf.shape[-2]
    slots = kv_buf.shape[0]
    heads = part // HEAD_DIM
    used = heads * block
    steps = owners

    def remote(src, dst, send, recv, ep=None, core=None):
        return pltpu.make_async_remote_copy(
            src_ref=src,
            dst_ref=dst,
            send_sem=send,
            recv_sem=recv,
            device_id={"ep": me if ep is None else ep, "rep": rep if core is None else core},
            device_id_type=pl.DeviceIdType.MESH,
        )

    def z_of(j):
        if cols == 4:
            k = 3 - j
            return (mz // 2 + k // 2) % 2 * 2 + (mz + k) % 2
        return (mz + 1 + j) % cols

    def second(s):
        t = (s + steps - 1) % steps
        return (1 - t % 2) * ((t + steps - 1) // steps) + t // (steps - 1)

    def turn_of(s):
        return ((s + steps - 1) % steps + 1) // 2 - second(s)

    def owner_of(s):
        return z_of(turn_of(s)) * 2 + (1 - mx + second(s)) % 2

    def kv_copy(s):
        return pltpu.make_async_copy(
            kv_hbm.at[:, owner_of(s)], kv_buf.at[s % slots], kv_sem.at[s % slots]
        )

    tiles = w_raw.shape[0]

    def raw_copy(n):
        return pltpu.make_async_copy(
            w_in_hbm.at[:, :, pl.ds(n * LANES, LANES)], w_raw.at[n], raw_sem.at[n]
        )

    down_copy = pltpu.make_async_copy(w_down_hbm, w_down_buf, w_sem)
    for s in range(slots):
        kv_copy(s).start()

    barrier = pltpu.get_barrier_semaphore()
    for i in range(1, owners):
        pl.semaphore_signal(
            barrier,
            inc=1,
            device_id={"ep": (me + i) % owners, "rep": rep},
            device_id_type=pl.DeviceIdType.MESH,
        )
    pl.semaphore_signal(
        barrier, inc=1, device_id={"ep": me, "rep": sister}, device_id_type=pl.DeviceIdType.MESH
    )
    pl.semaphore_wait(barrier, owners)

    def lanes_of(owner):
        return pl.ds(pl.multiple_of(owner * part, part), part)

    def q_copy(to, slot):
        return remote(
            qkv_ref.at[pl.ds(0, 1), :, lanes_of(to)],
            q_buf.at[slot, pl.ds(0, 1)],
            q_send.at[to],
            q_recv.at[slot],
            ep=to,
        )

    def v_copy(to, slot):
        return remote(
            qkv_ref.at[pl.ds(2, 1), :, lanes_of(to)],
            q_buf.at[slot, pl.ds(1, 1)],
            v_send.at[to],
            v_recv.at[slot],
            ep=to,
        )

    def own_copy(to, slot):
        return remote(
            own_out.at[to], own_in.at[slot], own_send.at[to], own_recv.at[slot], ep=to
        )

    for s in range(1, steps):
        q_copy(owner_of(s), me).start()
    for s in range(1, steps):
        v_copy(owner_of(s), me).start()

    head_of = lax.broadcasted_iota(jnp.int32, (block, part), 1) // HEAD_DIM
    scale = 1.0 / math.sqrt(HEAD_DIM)
    nt = (((1,), (1,)), ((), ()))
    diag = lax.broadcasted_iota(jnp.int32, (block, LANES), 0) == (
        lax.broadcasted_iota(jnp.int32, (block, LANES), 1) % block
    )

    def stacked(query):
        zero = jnp.zeros_like(query)
        stack = [jnp.where(head_of == h, query, zero) for h in range(heads)]
        stack += [zero] * (LANES // block - heads)
        return jnp.concatenate(stack, axis=0)

    for i in range(owners):
        lanes = slice(i * part, (i + 1) * part)
        fresh = lax.dot_general(
            qkv_ref[1, :, lanes], stacked(qkv_ref[0, :, lanes]), nt, preferred_element_type=F32
        )
        own = jnp.sum(jnp.where(diag, fresh, 0.0), axis=0, keepdims=True) * scale
        own_out[i] = jnp.broadcast_to(own, own_out.shape[1:])
    for s in range(1, steps):
        own_copy(owner_of(s), me).start()
    own_in[me] = own_out[me]
    q_buf[me, 0] = qkv_ref[0, :, lanes_of(me)]
    q_buf[me, 1] = qkv_ref[2, :, lanes_of(me)]

    flat = w_raw.reshape(tiles, 2 * width, LANES)
    chunk = 2 * LANES
    pick_row = lax.broadcasted_iota(jnp.int32, (chunk, chunk), 0)
    pick_col = lax.broadcasted_iota(jnp.int32, (chunk, chunk), 1)
    pick = jnp.where(
        pick_col == pick_row % LANES * 2 + pick_row // LANES, 1.0, 0.0
    ).astype(BF16)
    turns = 2 * width // chunk
    unroll = 4

    def planes(low, high):
        @pl.loop(low, high)
        def _(turn):
            for n in range(0, tiles, 2):
                many = min(2, tiles - n)
                for k in range(unroll):
                    i = turn * unroll + k
                    raw_rows = pl.ds(pl.multiple_of(i * chunk, chunk), chunk)
                    out_rows = pl.ds(pl.multiple_of(i * LANES, LANES), LANES)
                    both = jnp.concatenate(
                        [flat[n + t, raw_rows, :] for t in range(many)], axis=1
                    )
                    split = jnp.dot(pick, both, preferred_element_type=F32).astype(BF16)
                    for t in range(many):
                        at = (n + t) * chunk
                        lanes = slice(t * LANES, (t + 1) * LANES)
                        w_in_buf[out_rows, at : at + LANES] = split[:LANES, lanes]
                        w_in_buf[out_rows, at + LANES : at + chunk] = split[LANES:, lanes]

    rounds = turns // unroll
    first, early = 0, rounds // 2

    is_live = lax.broadcasted_iota(jnp.int32, (block, 1), 0) < count_ref[0]
    expert_id = lax.broadcasted_iota(jnp.int32, (LANES, LANES), 0)
    gates = gate_ref[...].astype(F32)
    ids = jnp.concatenate([ids_ref[...]] * (LANES // block), axis=1)
    gates = jnp.concatenate([gates] * (LANES // block), axis=1)
    coef = jnp.zeros((LANES, LANES), F32)
    for k in range(TOPK):
        coef += jnp.where(expert_id == ids[k : k + 1], gates[k : k + 1], 0.0)
    coef = coef.T[:block]
    rows_all[mx, rep, mz, :, width:] = jnp.where(is_live, coef, 0.0).astype(BF16)

    lane_row = lax.broadcasted_iota(jnp.int32, (1, LANES), 1) % block
    pos_of = lax.broadcasted_iota(jnp.int32, (positions, LANES), 0)
    row_mod = lax.broadcasted_iota(jnp.int32, (used, positions), 0) % block
    group = 8

    def partial(s):
        owner, slot = owner_of(s), s % slots

        @pl.when(owner != me)
        def _():
            q_copy(owner, owner).wait_recv()

        kv_copy(s).wait()
        queries = stacked(q_buf[owner, 0])

        scores = jnp.zeros((positions, LANES), F32)
        for g in range(block // group):
            keys = kv_buf[slot, 0, g * group : (g + 1) * group].reshape(group * positions, part)
            got = lax.dot_general(keys, queries, nt, preferred_element_type=F32)
            for r in range(group):
                scores = jnp.where(
                    lane_row == g * group + r, got[r * positions : (r + 1) * positions], scores
                )

        @pl.when(owner != me)
        def _():
            own_copy(owner, owner).wait_recv()

        own = own_in[owner][:1]
        lens = jnp.concatenate([lens_ref[pl.ds(owner, 1), :]] * (LANES // block), axis=1)
        in_cache = pos_of < lens
        scores = jnp.where(in_cache, scores * scale, masked_score)
        top = jnp.maximum(jnp.max(scores, axis=0, keepdims=True), own)
        weights = jnp.where(in_cache, jnp.exp(scores - top), 0.0)
        own_w = jnp.exp(own - top)
        den = jnp.sum(weights, axis=0, keepdims=True) + own_w
        own_t = jnp.broadcast_to(own_w, (LANES, LANES)).T
        den_t = jnp.broadcast_to(den, (LANES, LANES)).T
        weights_t = weights.T[:used]

        summed = jnp.zeros((used, part), F32)
        for g in range(block // group):
            wide = jnp.concatenate(
                [
                    jnp.where(row_mod == g * group + r, weights_t, 0.0).astype(BF16)
                    for r in range(group)
                ],
                axis=1,
            )
            values = kv_buf[slot, 1, g * group : (g + 1) * group].reshape(group * positions, part)
            summed += jnp.dot(wide, values, preferred_element_type=F32)

        @pl.when(s + slots < steps)
        def _():
            kv_copy(s + slots).start()

        @pl.when(owner != me)
        def _():
            v_copy(owner, owner).wait_recv()

        fresh_v = q_buf[owner, 1].astype(F32)
        pieces = []
        for h in range(heads):
            rows = slice(h * block, (h + 1) * block)
            lanes = slice(h * HEAD_DIM, (h + 1) * HEAD_DIM)
            pieces.append((summed[rows, lanes] + own_t[rows] * fresh_v[:, lanes]) / den_t[rows])
        attended = jnp.concatenate(pieces, axis=1).astype(BF16)
        return jnp.dot(attended, w_out_ref[...], preferred_element_type=F32)

    def pair_copy(z):
        return remote(pair_out.at[z], pair_in.at[z], pair_send.at[z], pair_recv.at[z], ep=across)

    def col_copy(z, slot):
        return remote(
            col_out.at[z], col_in.at[slot], col_send.at[z], col_recv.at[slot], ep=z * 2 + mx
        )

    @pl.loop(0, steps)
    def _(s):
        j = turn_of(s)
        z = z_of(j)
        made = partial(s)

        @pl.when(second(s) == 0)
        def _():
            pair_out[z] = made.astype(BF16)
            pair_copy(z).start()

        @pl.when(s == 1)
        def _():
            for n in range(tiles):
                raw_copy(n).start()

        @pl.when(s == steps - 1)
        def _():
            down_copy.start()

        @pl.when((second(s) == 1) & (s > 0))
        def _():
            pair_copy(z).wait_recv()
            col_out[z] = (made + pair_in[z].astype(F32)).astype(BF16)
            col_copy(z, mz).start()

        @pl.when(s == 0)
        def _():
            total[...] = made

    for n in range(tiles):
        raw_copy(n).wait()
    planes(first, early)
    pair_copy(mz).wait_recv()
    total[...] += pair_in[mz].astype(F32)

    for j in range(cols - 1):
        z = z_of(j)
        col_copy(z, z).wait_recv()
        total[...] += col_in[z].astype(F32)
    residual = (hidden_ref[...].astype(F32) + total[...]).astype(BF16)
    wide = residual.astype(F32)
    total[...] = wide
    inverse = lax.rsqrt(jnp.mean(wide * wide, axis=1, keepdims=True) + epsilon)
    rows_all[mx, rep, mz, :, :width] = (wide * inverse * gain_ref[...]).astype(BF16)

    cut = g_recv.shape[-1]
    bit = block // cut

    def row_copy(e, side, h, send, ep=None, core=None):
        at = rows_all.at[e % 2, side, e // 2, pl.ds(h * bit, bit)]
        return remote(at, at, send, g_recv.at[e % 2, side, e // 2, h], ep=ep, core=core)

    def up_copy(z, h):
        return row_copy(z * 2 + mx, rep, h, up_send.at[z, h], ep=me + 2)

    def lower_copy(z, h):
        return row_copy(z * 2 + mx, rep, h, down_send.at[z, h], ep=me - 2)

    def x_copy(e, h):
        return row_copy(e, rep, h, x_send.at[e, h], ep=across)

    def s_copy(e, side, h):
        return row_copy(e, side, h, s_send.at[e, h], core=sister)

    def send_up(z, h):
        @pl.when(mz < cols - 1)
        def _():
            up_copy(z, h).start()

    def send_down(z, h):
        @pl.when(mz > 0)
        def _():
            lower_copy(z, h).start()

    for h in range(cut):
        send_up(mz, h)
        send_down(mz, h)
        x_copy(me, h).start()
        s_copy(me, rep, h).start()
    planes(early, rounds * 3 // 4)
    for d in range(1, cols):
        if d == min(2, cols - 1):
            planes(rounds * 3 // 4, rounds)
        for h in range(cut):

            @pl.when(mz - d >= 0)
            def _():
                z = mz - d
                x_copy(z * 2 + mx, h).wait_recv()
                send_up(z, h)
                x_copy(z * 2 + mx, h).start()
                s_copy(z * 2 + mx, rep, h).start()

            @pl.when(mz + d < cols)
            def _():
                z = mz + d
                x_copy(z * 2 + mx, h).wait_recv()
                send_down(z, h)
                x_copy(z * 2 + mx, h).start()
                s_copy(z * 2 + mx, rep, h).start()

    expert = me * 2 + rep
    half = owners * block
    step = 4 * LANES

    def gate_up(x, low, high):
        def some(at, many):
            rows = rows_all[x, :, :, :, :width].reshape(half, width)
            both = jnp.dot(
                rows,
                w_in_buf[:, pl.ds(pl.multiple_of(at * chunk, chunk), many * chunk)],
                preferred_element_type=F32,
            )
            for t in range(many):
                gate = both[:, t * chunk : t * chunk + LANES]
                up = both[:, t * chunk + LANES : (t + 1) * chunk]
                lanes = pl.ds(pl.multiple_of((at + t) * LANES, LANES), LANES)
                hidden_buf[x, :, lanes] = (gate / (1.0 + jnp.exp(-gate)) * up).astype(BF16)

        pairs = (high - low) // 2

        @pl.loop(0, pairs)
        def _(n):
            some(low + 2 * n, 2)

        if low + 2 * pairs < high:
            some(high - 1, 1)

    turns_down = width // step // 2
    span = width // 2

    def down(x, f):
        coefs = rows_all[x, :, :, :, width:].reshape(half, LANES).astype(F32)
        lane = lax.broadcasted_iota(jnp.int32, (half, LANES), 1)
        factor = jnp.sum(jnp.where(lane == expert, coefs, 0.0), axis=1, keepdims=True)

        @pl.loop(f * turns_down, (f + 1) * turns_down)
        def _(n):
            lanes = pl.ds(pl.multiple_of(n * step, step), step)
            made = jnp.dot(hidden_buf[x], w_down_buf[:, lanes], preferred_element_type=F32)
            made = made.astype(BF16).astype(F32) * factor
            y_all[x, :, :, :, lanes] = made.astype(BF16).reshape(2, cols, block, step)

    def y_copy(x, z, f):
        lanes = pl.ds(f * span, span)
        return remote(
            y_all.at[x, sister, z, :, lanes],
            y_in.at[x, z, :, lanes],
            y_send.at[x, z, f],
            y_recv.at[x, z, f],
            core=sister,
        )

    def across_arrive(d):
        for h in range(cut):

            @pl.when(mz - d >= 0)
            def _():
                e = (mz - d) * 2 + 1 - mx
                x_copy(e, h).wait_recv()
                s_copy(e, rep, h).start()

            if d:

                @pl.when(mz + d < cols)
                def _():
                    e = (mz + d) * 2 + 1 - mx
                    x_copy(e, h).wait_recv()
                    s_copy(e, rep, h).start()

    def sister_arrive(x):
        for z in range(cols):
            for h in range(cut):
                s_copy(z * 2 + x, sister, h).wait_recv()

    sister_arrive(mx)
    gate_up(mx, 0, tiles // 4 * 2)
    for d in range(cols - 1):
        across_arrive(d)
    gate_up(mx, tiles // 4 * 2, tiles // 4 * 4)
    across_arrive(cols - 1)
    gate_up(mx, tiles // 4 * 4, tiles)
    down_copy.wait()
    sister_arrive(1 - mx)
    gate_up(1 - mx, 0, tiles)
    for f in range(2):
        down(1 - mx, f)
        for j in range(cols):
            y_copy(1 - mx, z_of(j), f).start()

    def pair_copy2(z, f):
        lanes = pl.ds(f * span, span)
        return remote(
            pair_out.at[z, :, lanes],
            pair_in.at[z, :, lanes],
            pair_send2.at[z, f],
            pair_recv2.at[z, f],
            ep=across,
        )

    def col_copy2(z, slot, f):
        lanes = pl.ds(f * span, span)
        return remote(
            col_out.at[z, :, lanes],
            col_in.at[slot, :, lanes],
            col_send2.at[z, f],
            col_recv2.at[slot, f],
            ep=z * 2 + mx,
        )

    for z in range(cols):
        pair_copy(z).wait_send()
    for j in range(cols - 1):
        col_copy(z_of(j), mz).wait_send()
    for f in range(2):
        lanes = slice(f * span, (f + 1) * span)
        for j in range(cols):
            z = z_of(j)
            y_copy(1 - mx, z, f).wait_recv()
            made = y_all[1 - mx, rep, z, :, lanes].astype(F32)
            made += y_in[1 - mx, z, :, lanes].astype(F32)
            pair_out[z, :, lanes] = made.astype(BF16)
            pair_copy2(z, f).start()
    for f in range(2):
        down(mx, f)
        for j in range(cols):
            y_copy(mx, z_of(j), f).start()
    for f in range(2):
        lanes = slice(f * span, (f + 1) * span)
        for j in range(cols):
            z = z_of(j)
            y_copy(mx, z, f).wait_recv()
            made = y_all[mx, rep, z, :, lanes].astype(F32) + y_in[mx, z, :, lanes].astype(F32)
            pair_copy2(z, f).wait_recv()
            mine = made + pair_in[z, :, lanes].astype(F32)
            if j < cols - 1:
                col_out[z, :, lanes] = mine.astype(BF16)
                col_copy2(z, mz, f).start()
            else:
                total[:, lanes] += mine
    for f in range(2):
        lanes = slice(f * span, (f + 1) * span)
        for j in range(cols - 1):
            z = z_of(j)
            col_copy2(z, z, f).wait_recv()
            total[:, lanes] += col_in[z, :, lanes].astype(F32)
        out_ref[:, lanes] = jnp.where(is_live, total[:, lanes], 0.0).astype(BF16)

    for s in range(1, steps):
        q_copy(owner_of(s), me).wait_send()
        v_copy(owner_of(s), me).wait_send()
        own_copy(owner_of(s), me).wait_send()
    for f in range(2):
        for z in range(cols):
            y_copy(0, z, f).wait_send()
            y_copy(1, z, f).wait_send()
            pair_copy2(z, f).wait_send()
        for j in range(cols - 1):
            col_copy2(z_of(j), mz, f).wait_send()
    for z in range(cols):
        for h in range(cut):
            x_copy(z * 2 + mx, h).wait_send()

    for z in range(cols):

        @pl.when((z <= mz) & (mz < cols - 1))
        def _():
            for h in range(cut):
                up_copy(z, h).wait_send()

        @pl.when((z >= mz) & (mz > 0))
        def _():
            for h in range(cut):
                lower_copy(z, h).wait_send()

    for e in range(owners):
        for h in range(cut):
            s_copy(e, rep, h).wait_send()


def fast_local(
    owners,
    hidden_in,
    row_counts,
    qkv_new,
    cache_len,
    kv_cache,
    w_out,
    moe_gain,
    w_in,
    w_down,
    route_ids,
    route_weight,
):
    block, width = hidden_in.shape
    part = kv_cache.shape[-1]
    positions = kv_cache.shape[3]
    cols = owners // 2
    inner = w_down.shape[1]
    tiles = inner // LANES
    fresh = jnp.transpose(qkv_new, (1, 0, 2))
    vmem = pl.BlockSpec(memory_space=pltpu.VMEM)
    hbm = pl.BlockSpec(memory_space=pl.ANY)
    smem = pl.BlockSpec(memory_space=pltpu.SMEM)
    dma = pltpu.SemaphoreType.DMA
    wide = (cols, block, width)
    slots = min(3, owners)
    cut = 2
    return pl.pallas_call(
        functools.partial(layer_kernel, owners),
        out_shape=jax.ShapeDtypeStruct((block, width), BF16),
        in_specs=[vmem, vmem, hbm, vmem, vmem, vmem, vmem, vmem, smem, hbm, hbm],
        out_specs=vmem,
        scratch_shapes=[
            pltpu.VMEM((slots, 2, block, positions, part), BF16),
            pltpu.VMEM((owners, 2, block, part), BF16),
            pltpu.VMEM((owners, 8, LANES), F32),
            pltpu.VMEM((owners, 8, LANES), F32),
            pltpu.VMEM(wide, BF16),
            pltpu.VMEM(wide, BF16),
            pltpu.VMEM(wide, BF16),
            pltpu.VMEM(wide, BF16),
            pltpu.VMEM((block, width), F32),
            pltpu.VMEM((2, 2, cols, block, width + LANES), BF16),
            pltpu.VMEM((tiles, width, 2, LANES), BF16),
            pltpu.VMEM((width, 2 * inner), BF16),
            pltpu.VMEM((inner, width), BF16),
            pltpu.VMEM((2, owners * block, inner), BF16),
            pltpu.VMEM((2, 2, cols, block, width), BF16),
            pltpu.VMEM((2, cols, block, width), BF16),
            dma((slots,)),
            dma((tiles,)),
            dma,
            dma((owners,)),
            dma((owners,)),
            dma((owners,)),
            dma((owners,)),
            dma((owners,)),
            dma((owners,)),
            dma((cols,)),
            dma((cols,)),
            dma((cols,)),
            dma((cols,)),
            dma((cols, cut)),
            dma((cols, cut)),
            dma((owners, cut)),
            dma((owners, cut)),
            dma((2, 2, cols, cut)),
            dma((2, cols, 2)),
            dma((2, cols, 2)),
            dma((cols, 2)),
            dma((cols, 2)),
            dma((cols, 2)),
            dma((cols, 2)),
        ],
        compiler_params=pltpu.CompilerParams(
            collective_id=0, has_side_effects=True, vmem_limit_bytes=63 * 1024 * 1024
        ),
    )(
        fresh,
        cache_len,
        kv_cache,
        w_out,
        hidden_in,
        moe_gain.reshape(1, width),
        route_ids.T,
        route_weight.T,
        row_counts,
        w_in.reshape(width, 2, inner),
        w_down.reshape(inner, width),
    )


def solution(mesh):
    placed = (
        P(("grp", "ep", "rep"), "seq"),
        P(("grp", "ep", "rep")),
        P(("grp", "ep", "rep"), None, None),
        P("grp", ("rep", "seq")),
        P(None, "grp", ("rep", "seq"), None, "ep"),
        P("ep", "seq"),
        P(),
        P(("ep", "rep"), None, None, "seq"),
        P(("ep", "rep"), "seq", None),
        P(("grp", "ep", "rep"), None),
        P(("grp", "ep", "rep"), None),
    )
    sizes = mesh.shape
    owners = sizes["ep"]
    one_step = sizes["seq"] == 1 and sizes["rep"] == 2 and owners in (4, 8)
    body = functools.partial(fast_local, owners) if one_step else local
    return jax.shard_map(
        body, mesh=mesh, in_specs=placed, out_specs=P(("grp", "ep", "rep"), "seq"), check_vma=False
    )
```
